32 devices in a mesh: tm: 8 (over z, y), obs: 4 (over x, core).
Axes of the slice: x: 2, y: 2, z: 4, core: 2. Of those that a mesh axis runs over, the one named last changes fastest.
Arguments:
- obs_rows: float32 [256, 768], P(('tm', 'obs')), may hold values from -6 to 6
- obs_owner: int32 [256, 1], P(('tm', 'obs')), may hold values from 0 to 7; in each aligned block of 8 rows (0 to 7, 8 to 15, ...) at most 2 rows name the same one
- obs_member: int32 [256, 1], P(('tm', 'obs')), may hold values from 0 to 7
- prior_diag: float32 [64, 384], P(('tm', 'obs')), may hold values from 1 to 4
- lower_coupling: float32 [64, 384, 384], P(('tm', 'obs')), may hold values from -2 to 2
- tip_coupling: float32 [64, 128, 384], P(('tm', 'obs')), may hold values from -0.095683193 to 0.095683193
- time_rhs: float32 [64, 384], P(('tm', 'obs')), may hold values from -6 to 6
- tip_prior: float32 [128], replicated, may hold values from 0.5 to 2
- tip_rhs: float32 [128], replicated, may hold values from -30 to 30
Outputs:
- reduced_block: float32 [64, 384, 384], P(('tm', 'obs'))
- reduced_lower: float32 [64, 384, 384], P(('tm', 'obs'))
- reduced_tip: float32 [64, 128, 384], P(('tm', 'obs'))
- time_result: float32 [64, 384], P(('tm', 'obs'))
- tip_solution: float32 [128], replicated
The draws below stay inside these ranges and needn't reach their ends.
Inputs may be any that keep to these rules, and one draw needn't show every extreme that they name: `obs_owner`: of the 8 observation blocks of one device, at most 2 name the same owner group, and in every draw some device has an owner group named exactly 2 times.
All inputs are finite; a program needn't handle non-finite values.
Results may differ from the reference program's by a relative error of at most 0.00016.
Values sent between devices are 32-bit elements; how exact they have to be, the bound alone decides.
A program may use at most 64 MiB of HBM per device.

```python
import math
import jax
import jax.numpy as jnp
import numpy as np
from jax import lax

B = 384
K = 128
R = 2
CAP = 2
NT = 64
OB_DEV = 8
N_TM = 8
N_OBS = 4


def draw_tip_coupling(key, part):
    base = jnp.clip(jax.random.normal(key, (NT, K, B), jnp.float32), -5.0, 5.0)
    ramp = 1.0 + 2.0 * jnp.arange(NT, dtype=jnp.float32)[:, None, None] / max(NT - 1, 1)
    return base * ramp / math.sqrt(NT * B)


def touch_ends(entries, stream_key, low, top_value):
    longest = entries.shape.index(max(entries.shape))
    spots = []
    for shift in (0, 1):
        where = [jax.random.randint(jax.random.fold_in(stream_key, axis), (), 0, length) for axis, length in enumerate(entries.shape)]
        where[longest] = (where[longest] + shift) % entries.shape[longest]
        spots.append(tuple(where))
    return entries.at[spots[0]].set(low).at[spots[1]].set(top_value)


def level_of(own_key, extent, pieces, low, high):
    level, own = 1.0, jax.random.fold_in(own_key, 6)
    for position, parts in pieces:
        steps = jnp.exp(jax.random.uniform(jax.random.fold_in(own, position), (parts,), jnp.float32, low / len(pieces), high / len(pieces)))
        level = level * jnp.repeat(steps, extent[position] // parts).reshape([-1 if axis == position else 1 for axis in range(len(extent))])
    return level


def deal_out(key, own, number, rows, amount, top, reach, slope):
    sequence = jax.random.permutation(key, amount)
    heavy_load, common = shares(amount, rows * top, reach, slope, True), shares(amount, rows * top, reach, slope, False)
    places = jnp.arange(amount)

    def named(lengths, turn):
        used = int((lengths > 0).sum())
        fixed = max(1, used // 4)
        shifted = fixed + (places - fixed + turn * (used - fixed)) % max(1, amount - fixed)
        return jnp.zeros((amount,), jnp.int32).at[sequence[jnp.where(places < fixed, places, shifted)]].set(jnp.asarray(lengths, jnp.int32))

    lengths = jnp.where(number % 4 == 0, named(heavy_load, number // 4), named(common, number - number // 4 - 1))
    mixed = jax.random.permutation(jax.random.fold_in(own, 3), amount)
    source_of, taker = mixed[0:amount // 2 * 2:2], mixed[1:amount // 2 * 2:2]
    margin = jnp.minimum(lengths[source_of] - 1, reach - lengths[taker]) // 2
    margin = jnp.where((source_of == sequence[0]) | (taker == sequence[0]) | (lengths[taker] == 0), 0, jnp.maximum(margin, 0))
    shifted = jax.random.randint(jax.random.fold_in(own, 4), (amount // 2,), 0, 1 << 20) % (margin + 1)
    lengths = lengths.at[source_of].add(-shifted).at[taker].add(shifted)
    labels = jnp.searchsorted(jnp.cumsum(lengths), jnp.arange(rows * top), side="right").astype(jnp.int32)
    table = labels.reshape(top, rows).T
    table = table[jax.random.permutation(jax.random.fold_in(own, 1), rows)]
    turn = jax.random.randint(jax.random.fold_in(own, 2), (rows, 1), 0, top)
    return jnp.take_along_axis(table, (jnp.arange(top)[None, :] + turn) % top, axis=1)


def shares(amount, total, limit, lean, full):
    loads = [(1 << 20) // math.isqrt(standing ** lean) + 1 for standing in range(1, amount + 1)]
    largest = limit if full else min(limit, max(-(-total // amount), total * loads[0] // sum(loads)))
    least = 1 if total - largest >= amount - 1 else 0
    given, rest = [largest] + [least] * (amount - 1), total - largest - least * (amount - 1)
    while rest > 0:
        candidates = [i for i in range(1, amount) if given[i] < largest] or [i for i in range(1, amount) if given[i] < limit]
        whole, budget = sum([loads[i] for i in candidates]), rest
        for i in candidates:
            addition = min(limit - given[i], max(1, budget * loads[i] // whole), rest)
            given[i] = given[i] + addition
            rest = rest - addition
    return np.array(given)


def bell_draw(own_key, dims, deviation, limit, shards=(), held_as=jnp.bfloat16):
    gain = level_of(own_key, dims, shards, -0.22, 0.18) if shards else 1.0
    values = jax.random.normal(own_key, dims, jnp.float32) * deviation * gain
    return jnp.minimum(jnp.maximum(values, -limit), limit).astype(held_as)


def setup_inputs(seed: int = 0) -> dict:
    key_list = jax.random.split(jax.random.key(seed), 10)
    obs_rows = bell_draw(key_list[0], (N_TM * N_OBS * OB_DEV, R * B), ((3.0 / (OB_DEV * R)) ** 0.5), 6.0, ((0, 32),), jnp.float32)
    obs_owner_keys = jax.random.split(jax.random.fold_in(key_list[1], 1), (N_TM * N_OBS * OB_DEV) // OB_DEV)
    obs_owner_turns = jax.random.permutation(jax.random.fold_in(key_list[1], 3), (N_TM * N_OBS * OB_DEV) // OB_DEV)
    obs_owner = jax.vmap(lambda own, number: deal_out(jax.random.fold_in(key_list[1], 2), own, number, OB_DEV, N_TM, 1, CAP, 2))(obs_owner_keys, obs_owner_turns).reshape((N_TM * N_OBS * OB_DEV, 1))
    obs_member = touch_ends(jax.random.randint(key_list[2], (N_TM * N_OBS * OB_DEV, 1), 0, 2 * N_OBS), jax.random.fold_in(key_list[2], 1), 0, (2 * N_OBS) - 1).astype(jnp.int32)
    prior_diag = jnp.clip(jnp.exp(math.log(4.0) - 1.3862944 * jax.random.uniform(key_list[3], (NT, B), jnp.float32) ** level_of(key_list[3], (NT, B), ((0, 32),), -0.2, 0.2)), 1.0, 4.0)
    lower_coupling = bell_draw(key_list[4], (NT, B, B), (3.0 / B ** 0.5), 2.0, ((0, 32),), jnp.float32)
    tip_coupling = draw_tip_coupling(jax.random.fold_in(key_list[9], 71), 0)
    time_rhs = bell_draw(key_list[6], (NT, B), 1.0, 6.0, ((0, 32),), jnp.float32)
    tip_prior = jnp.clip(jnp.exp(jax.random.uniform(key_list[7], (K,), jnp.float32, math.log(0.5), math.log(2.0))), 0.5, 2.0)
    tip_rhs = bell_draw(key_list[8], (K,), 5.0, 30.0, (), jnp.float32)
    return {"obs_rows": obs_rows, "obs_owner": obs_owner, "obs_member": obs_member, "prior_diag": prior_diag, "lower_coupling": lower_coupling, "tip_coupling": tip_coupling, "time_rhs": time_rhs, "tip_prior": tip_prior, "tip_rhs": tip_rhs}


FULL_PRECISION = lax.Precision.HIGHEST

def solve_lower(factor, right, transpose=False):
    return lax.linalg.triangular_solve(factor, right, left_side=True, lower=True, transpose_a=transpose)

def reference(obs_rows, obs_owner, obs_member, prior_diag, lower_coupling, tip_coupling, time_rhs, tip_prior, tip_rhs):
    target = (obs_owner[:, 0] * (2 * N_OBS) + obs_member[:, 0]).astype(jnp.int32)
    block_total = obs_rows.shape[0]
    batch_size = 64
    row_batches = obs_rows.reshape(block_total // batch_size, batch_size, R, B)
    target_batches = target.reshape(block_total // batch_size, batch_size)

    def add_blocks(grams, item):
        batch_rows, batch_targets = item
        products = jnp.einsum('jrb,jrc->jbc', batch_rows, batch_rows, precision=FULL_PRECISION)
        return (grams.at[batch_targets].add(products), None)
    grams, _ = lax.scan(add_blocks, jnp.zeros((NT, B, B), jnp.float32), (row_batches, target_batches))
    identity = jnp.eye(B, dtype=jnp.float32)
    blocks_all = grams + prior_diag[:, :, None] * identity
    first_mask = (jnp.arange(NT) == 0)[:, None, None]
    low = jnp.where(first_mask, jnp.zeros_like(lower_coupling), lower_coupling)
    even_blocks = blocks_all[0::2]
    odd_blocks = blocks_all[1::2]
    factor = jnp.linalg.cholesky(even_blocks)
    fill_block = solve_lower(factor, low[0::2])
    tip_side = solve_lower(factor, jnp.swapaxes(tip_coupling[0::2], 1, 2))
    lifted = solve_lower(factor, time_rhs[0::2][:, :, None])[:, :, 0]
    left_cross = solve_lower(factor, jnp.swapaxes(low[1::2], 1, 2))
    right_fill = jnp.concatenate([fill_block[1:], jnp.zeros_like(fill_block[:1])], axis=0)
    right_side = jnp.concatenate([tip_side[1:], jnp.zeros_like(tip_side[:1])], axis=0)
    right_lift = jnp.concatenate([lifted[1:], jnp.zeros_like(lifted[:1])], axis=0)

    def pair_product(left, right):
        return jnp.einsum('ibk,ibc->ikc', left, right, precision=FULL_PRECISION)
    odd_reduced = odd_blocks - pair_product(left_cross, left_cross) - pair_product(right_fill, right_fill)
    odd_lower = -pair_product(left_cross, fill_block)
    odd_tip = tip_coupling[1::2] - pair_product(tip_side, left_cross) - pair_product(right_side, right_fill)
    odd_rhs = time_rhs[1::2] - jnp.einsum('ibc,ib->ic', left_cross, lifted, precision=FULL_PRECISION) - jnp.einsum('ibc,ib->ic', right_fill, right_lift, precision=FULL_PRECISION)
    schur_block = jnp.diag(tip_prior) + jnp.einsum('tkb,tjb->kj', tip_coupling, tip_coupling, precision=FULL_PRECISION) - jnp.einsum('ibk,ibj->kj', tip_side, tip_side, precision=FULL_PRECISION)
    tip_vec = tip_rhs - jnp.einsum('ibk,ib->k', tip_side, lifted, precision=FULL_PRECISION)
    chol_tip = jnp.linalg.cholesky(schur_block)
    halfway = solve_lower(chol_tip, tip_vec[:, None])
    tip_solution = solve_lower(chol_tip, halfway, True)[:, 0]
    pulled = lifted - jnp.einsum('ibk,k->ib', tip_side, tip_solution, precision=FULL_PRECISION)
    estimate = solve_lower(factor, pulled[:, :, None], True)[:, :, 0]

    def weave(even_part, odd_part):
        return jnp.stack([even_part, odd_part], axis=1).reshape((NT,) + even_part.shape[1:])
    reduced_block = weave(factor, odd_reduced)
    reduced_lower = weave(fill_block, odd_lower)
    reduced_tip = weave(jnp.swapaxes(tip_side, 1, 2), odd_tip)
    time_result = weave(estimate, odd_rhs)
    return (reduced_block, reduced_lower, reduced_tip, time_result, tip_solution)
```

```python
import jax
import jax.numpy as jnp
from jax import lax
from jax.experimental import pallas as pl
from jax.experimental.pallas import tpu as pltpu
from jax.sharding import PartitionSpec as P

R = 2
CAP = 2
T = 128
PANEL = 16
SUB = 8
HI = lax.Precision.HIGHEST
VMEM = pl.BlockSpec(memory_space=pltpu.VMEM)
ANY = pl.BlockSpec(memory_space=pl.ANY)
MESH = pl.DeviceIdType.MESH
NN = (((1,), (0,)), ((), ()))
NT = (((1,), (1,)), ((), ()))
TN = (((0,), (0,)), ((), ()))


def dot(a, b, dims):
    return lax.dot_general(a, b, dims, precision=HI, preferred_element_type=jnp.float32)


def split2(x):
    h = x.astype(jnp.bfloat16)
    return h, (x - h.astype(jnp.float32)).astype(jnp.bfloat16)


def split3(x):
    h = x.astype(jnp.bfloat16)
    rest = x - h.astype(jnp.float32)
    m = rest.astype(jnp.bfloat16)
    return h, m, (rest - m.astype(jnp.float32)).astype(jnp.bfloat16)


def mm3(a, b, dims):
    (ca,), (cb,) = dims[0]
    left = jnp.concatenate([a[0], a[1], a[0]], axis=ca)
    right = jnp.concatenate([b[0], b[0], b[1]], axis=cb)
    return lax.dot_general(left, right, dims, preferred_element_type=jnp.float32)


def panel_gram(rows):
    h, m, l = split3(rows)
    left = jnp.concatenate([part[:, :T] for part in (h, h, m, h, l, m)], axis=0)
    right = jnp.concatenate([h, m, h, l, h, m], axis=0)
    return lax.dot_general(left, right, TN, preferred_element_type=jnp.float32)


def spread(x, i):
    return jnp.broadcast_to(x[i : i + 1, :], x.shape)


def eliminate(rows, base):
    groups = PANEL // SUB
    sub = lax.broadcasted_iota(jnp.int32, (SUB, T), 0)
    lane = lax.broadcasted_iota(jnp.int32, (SUB, T), 1)
    left = [rows[SUB * g : SUB * (g + 1), :T] for g in range(groups)]
    right = [rows[SUB * g : SUB * (g + 1), T:] for g in range(groups)]
    cols = [
        [
            jnp.broadcast_to(jnp.sum(jnp.where(lane == base + j, x, 0.0), axis=1, keepdims=True), (SUB, T))
            for x in left
        ]
        for j in range(PANEL)
    ]
    scale = [jnp.zeros((SUB, T), jnp.float32) for _ in range(groups)]
    for i in range(0, PANEL, 2):
        first, s = i // SUB, i % SUB
        a = spread(cols[i][first], s)
        b = spread(cols[i + 1][first], s)
        c = spread(cols[i + 1][first], s + 1)
        det = a * c - b * b
        inv_det, inv_a = 1.0 / det, 1.0 / a
        scale[first] = jnp.where(
            sub == s, lax.rsqrt(a), jnp.where(sub == s + 1, lax.rsqrt(det * inv_a), scale[first])
        )
        l1, l2 = spread(left[first], s), spread(left[first], s + 1)
        r1, r2 = spread(right[first], s), spread(right[first], s + 1)
        heads = {j: (spread(cols[j][first], s), spread(cols[j][first], s + 1)) for j in range(i + 2, PANEL)}
        for g in range(first, groups):
            ci, cj = cols[i][g], cols[i + 1][g]
            n1, n2 = c * ci - b * cj, a * cj - b * ci
            if g == first:
                n1, n2 = jnp.where(sub > s + 1, n1, 0.0), jnp.where(sub > s + 1, n2, 0.0)
            m1, m2 = n1 * inv_det, n2 * inv_det
            if g > first or s + 2 < SUB:
                for j in range(i + 2, PANEL):
                    cols[j][g] = cols[j][g] - m1 * heads[j][0] - m2 * heads[j][1]
            if g == first:
                m1 = jnp.where(sub == s + 1, b * inv_a, m1)
            left[g] = left[g] - m1 * l1 - m2 * l2
            right[g] = right[g] - m1 * r1 - m2 * r2
    return jnp.concatenate(
        [jnp.concatenate([left[g] * scale[g], right[g] * scale[g]], axis=1) for g in range(groups)], axis=0
    )


def factor_tiles(works):
    row = lax.broadcasted_iota(jnp.int32, (T, 2 * T), 0)

    def body(p, carry):
        base = pl.multiple_of(p * PANEL, PANEL)
        done = [eliminate(work[pl.ds(base, PANEL), :], base) for work in works]
        for work, rows in zip(works, done):
            work[pl.ds(base, PANEL), :] = rows
        for work, rows in zip(works, done):
            work[...] = jnp.where(row >= base + PANEL, work[...] - panel_gram(rows), work[...])
        return carry

    lax.fori_loop(0, T // PANEL, body, 0)


def eye(n):
    return (
        lax.broadcasted_iota(jnp.int32, (n, n), 0) == lax.broadcasted_iota(jnp.int32, (n, n), 1)
    ).astype(jnp.float32)


def upper_mask(n):
    return lax.broadcasted_iota(jnp.int32, (n, n), 0) <= lax.broadcasted_iota(jnp.int32, (n, n), 1)


def pack(rows_ref, owner_ref, member_ref, out_ref):
    groups = out_ref.shape[0]
    blocks, width = rows_ref.shape
    owners = owner_ref[...]
    named = (lax.broadcasted_iota(jnp.int32, (groups, blocks), 0) == owners).astype(jnp.float32)
    before = lax.broadcasted_iota(jnp.int32, (blocks, blocks), 0) < lax.broadcasted_iota(
        jnp.int32, (blocks, blocks), 1
    )
    rank = jnp.sum(dot(named, before.astype(jnp.float32), NN) * named, axis=0, keepdims=True)
    slot = owners.astype(jnp.float32) * CAP + rank
    spots = lax.broadcasted_iota(jnp.int32, (groups * CAP, blocks), 0).astype(jnp.float32)
    pick = (spots == slot).astype(jnp.float32)
    rows = dot(pick, rows_ref[...], NN)
    tag = jnp.sum(pick * (member_ref[...].astype(jnp.float32) + 1.0), axis=1, keepdims=True)
    tags = jnp.broadcast_to(tag, (groups * CAP, T))
    for g in range(groups):
        out_ref[g, :, :width] = rows[g * CAP : (g + 1) * CAP, :]
        out_ref[g, :, width:] = tags[g * CAP : (g + 1) * CAP, :]


def main_kernel(
    rows_ref, owner_ref, member_ref, prior_ref, lower_ref, tip_ref, rhs_ref,
    l_ref, w_ref, y_ref, blk_ref, odd_ref, part_ref, back_ref, sum_ref, nw_ref, ny_ref,
    lower, tip, outgoing, stage, landed, even_rows, odd_rows, gram, work, work_k, flat, parts, base_ref,
    local_sem, send_a, recv_a, send_b, recv_b, send_c, recv_c, send_d, recv_d, send_e, recv_e,
):
    groups, n_obs = lax.axis_size("tm"), lax.axis_size("obs")
    n = groups * n_obs
    t, o = lax.axis_index("tm"), lax.axis_index("obs")
    me = t * n_obs + o
    B = prior_ref.shape[1]
    K = tip_ref.shape[1]
    nb = B // T
    chunks = (K + SUB) // SUB
    count = n * CAP * R
    early = count <= T

    def device(k):
        return (k // n_obs, lax.rem(k, n_obs))

    def remote(src, dst, send, recv, where):
        return pltpu.make_async_remote_copy(
            src_ref=src, dst_ref=dst, send_sem=send, recv_sem=recv, device_id=where, device_id_type=MESH
        )

    def toward(k):
        peer = lax.rem(t + k, groups)
        return remote(outgoing.at[peer], stage.at[k], send_a.at[k], recv_a.at[k], (peer, o))

    def across(k, j):
        slot = k * n_obs + j
        return remote(stage.at[k], landed.at[j, k], send_b.at[slot], recv_b.at[slot], (t, lax.rem(o + j, n_obs)))

    def reducer(i):
        return i * n // chunks

    mine = (me * chunks + n - 1) // n
    reducing = jnp.logical_and(mine < chunks, reducer(mine) == me)

    def rows_of(i):
        return pl.ds(pl.multiple_of(i * SUB, SUB), SUB)

    def scatter(i):
        return remote(flat.at[rows_of(i)], parts.at[me], send_c.at[i], recv_c.at[me], device(reducer(i)))

    def arrive(k):
        return remote(flat.at[rows_of(0)], parts.at[k], send_c.at[0], recv_c.at[k], device(k))

    def gather(k):
        return remote(sum_ref.at[rows_of(mine)], sum_ref.at[rows_of(mine)], send_d.at[k], recv_d.at[mine], device(k))

    def collect(i):
        return remote(sum_ref.at[rows_of(i)], sum_ref.at[rows_of(i)], send_d.at[0], recv_d.at[i], device(reducer(i)))

    def shift(b):
        where = device(lax.rem(me + n - 1, n))
        rows, lanes = pl.ds(b * T, T), pl.ds(b * T, T)
        return (
            remote(w_ref.at[rows], nw_ref.at[rows], send_e.at[2 * b], recv_e.at[2 * b], where),
            remote(
                y_ref.at[pl.ds(B, K + SUB), lanes], ny_ref.at[:, lanes],
                send_e.at[2 * b + 1], recv_e.at[2 * b + 1], where,
            ),
        )

    barrier = pltpu.get_barrier_semaphore()

    @pl.loop(1, n)
    def _(k):
        pl.semaphore_signal(barrier, inc=1, device_id=device(lax.rem(me + k, n)), device_id_type=MESH)

    load_tip = pltpu.make_async_copy(tip_ref, tip, local_sem.at[0])
    load_low = pltpu.make_async_copy(lower_ref.at[0], lower, local_sem.at[1])
    load_cross = pltpu.make_async_copy(lower_ref.at[1], y_ref.at[pl.ds(0, B)], local_sem.at[2])
    load_tip.start()
    load_low.start()
    load_cross.start()
    pack(rows_ref, owner_ref, member_ref, outgoing)
    pl.semaphore_wait(barrier, n - 1)

    @pl.loop(1, groups)
    def _(k):
        toward(k).start()

    own = pltpu.make_async_copy(outgoing.at[t], stage.at[0], local_sem.at[3])
    own.start()
    own.wait()
    for j in range(1, n_obs):
        across(0, j).start()

    @pl.loop(1, groups)
    def _(k):
        toward(k).wait_recv()
        for j in range(1, n_obs):
            across(k, j).start()

    load_tip.wait()
    load_low.wait()
    load_cross.wait()
    w_ref[...] = jnp.where(me == 0, 0.0, lower[...])
    y_ref[B : B + K, :] = tip[0]
    rhs8 = jnp.concatenate([rhs_ref[0:1, :], jnp.zeros((SUB - 1, B), jnp.float32)], axis=0)
    y_ref[B + K :, :] = rhs8
    root = lax.rsqrt(prior_ref[0:1, :])
    scaled = y_ref[B:, :] * root
    both = dot(tip[0], tip[0], NT) + dot(tip[1], tip[1], NT)
    if early:
        inner = dot(scaled, scaled[:K], NT)
        base_ref[:K, :] = both - inner[:K]
        base_ref[K:, :] = inner[K:]
    else:
        base_ref[:K, :] = both
        base_ref[K:, :] = jnp.zeros((SUB, K), jnp.float32)
    l_ref[...] = jnp.zeros((B, B), jnp.float32)

    @pl.when(me == n - 1)
    def _():
        nw_ref[...] = jnp.zeros((B, B), jnp.float32)
        ny_ref[...] = jnp.zeros((K + SUB, B), jnp.float32)

    for j in range(1, n_obs):

        @pl.loop(0, groups)
        def _(k):
            across(k, j).wait_recv()

    even = (2 * o + 1).astype(jnp.float32)
    odd = even + 1.0
    each = SUB // CAP
    pieces = [(j, k) for j in range(n_obs) for k in range(groups)]
    for q in range(0, n, each):
        block = jnp.concatenate([landed[j, k] if j else stage[k] for j, k in pieces[q : q + each]], axis=0)
        tag = block[:, R * B :]
        for r in range(R):
            at = r * n * CAP + q * CAP
            for c in range(nb):
                x = block[:, r * B + c * T : r * B + (c + 1) * T]
                even_rows[at : at + SUB, c * T : (c + 1) * T] = jnp.where(tag == even, x, 0.0)
                odd_rows[at : at + SUB, c * T : (c + 1) * T] = jnp.where(tag == odd, x, 0.0)
    chosen = even_rows[...]
    gram[...] = dot(chosen, chosen, TN) + prior_ref[0:1, :] * eye(B)
    if early:
        weighed = chosen * root
        if count < T:
            weighed = jnp.concatenate([weighed, jnp.zeros((T - count, B), jnp.float32)], axis=0)
        work_k[:, :T] = dot(weighed, weighed, NT) + eye(T)
        work_k[:, T:] = eye(T)
        crossed = dot(scaled, weighed, NT)

    def send_terms():
        @pl.loop(0, chunks)
        def _(i):
            @pl.when(reducer(i) != me)
            def _():
                scatter(i).start()

    def combine():
        @pl.when(reducing)
        def _():
            parts[me] = flat[rows_of(mine)]

            @pl.loop(0, n)
            def _(k):
                @pl.when(k != me)
                def _():
                    arrive(k).wait_recv()

            total = parts[0]
            if n <= 64:
                for k in range(1, n):
                    total = total + parts[k]
            else:
                total = lax.fori_loop(1, n, lambda k, acc: acc + parts[k], total)
            sum_ref[rows_of(mine)] = total

            @pl.loop(0, n)
            def _(k):
                @pl.when(k != me)
                def _():
                    gather(k).start()

    upper = upper_mask(T)
    inverse = []
    for b in range(nb):
        lo, hi = b * T, (b + 1) * T
        work[:, :T] = gram[lo:hi, lo:hi]
        work[:, T:] = eye(T)
        if b == 0 and early:
            factor_tiles([work, work_k])
            side = dot(crossed, jnp.where(upper.T, work_k[:, T:], 0.0), NT)
            seen = dot(side, side[:K], NT)
            flat[:K, :] = base_ref[:K, :] + seen[:K]
            flat[K:, :] = base_ref[K:, :] - seen[K:]
            send_terms()
        else:
            factor_tiles([work])
        inv_b = jnp.where(upper.T, work[:, T:], 0.0)
        inv_s = split2(inv_b)
        inverse.append(inv_s)
        l_ref[lo:hi, lo:hi] = jnp.where(upper, work[:, :T], 0.0).T
        w_b = mm3(inv_s, split2(w_ref[lo:hi, :]), NN)
        w_ref[lo:hi, :] = w_b
        y_b = mm3(split2(y_ref[:, lo:hi]), inv_s, NT)
        y_ref[:, lo:hi] = y_b

        @pl.when(me > 0)
        def _():
            for copy in shift(b):
                copy.start()

        if b + 1 < nb:
            rest = dot(inv_b, gram[lo:hi, hi:], NN)
            gram[hi:, hi:] = gram[hi:, hi:] - dot(rest, rest, TN)
            l_ref[hi:, lo:hi] = rest.T
            rest_s = split2(rest)
            w_ref[hi:, :] = w_ref[hi:, :] - mm3(rest_s, split2(w_b), TN)
            y_ref[:, hi:] = y_ref[:, hi:] - mm3(split2(y_b), rest_s, NN)
        if b == 1 and early:
            combine()
    if not early:
        side = y_ref[B:, :]
        seen = dot(side, side[:K], NT)
        flat[:K, :] = base_ref[:K, :] - seen[:K]
        flat[K:, :] = seen[K:]
        send_terms()
    if not early or nb < 2:
        combine()
    y_s = split2(y_ref[...])
    x_s = tuple(part[:B] for part in y_s)
    back = mm3(y_s, x_s, NT)
    chosen = odd_rows[...]
    blk_ref[...] = dot(chosen, chosen, TN) + prior_ref[1:2, :] * eye(B) - back[:B]
    part_ref[:K, :] = tip[1] - back[B : B + K]
    part_ref[K:, :] = rhs_ref[1:2, :] - back[B + K :]
    odd_ref[...] = -mm3(x_s, split2(w_ref[...]), NN)
    for b in reversed(range(nb)):
        lo, hi = b * T, (b + 1) * T
        value = y_ref[B:, lo:hi]
        if hi < B:
            value = value - mm3(split2(back_ref[:, hi:]), split2(l_ref[hi:, lo:hi]), NN)
        back_ref[:, lo:hi] = mm3(split2(value), inverse[b], NN)

    @pl.loop(0, chunks)
    def _(i):
        @pl.when(reducer(i) != me)
        def _():
            collect(i).wait_recv()

    @pl.when(me < n - 1)
    def _():
        for b in range(nb):
            for copy in shift(b):
                copy.wait_recv()

    @pl.when(me > 0)
    def _():
        for b in range(nb):
            for copy in shift(b):
                copy.wait_send()

    @pl.loop(0, chunks)
    def _(i):
        @pl.when(reducer(i) != me)
        def _():
            scatter(i).wait_send()

    @pl.when(reducing)
    def _():
        @pl.loop(0, n)
        def _(k):
            @pl.when(k != me)
            def _():
                gather(k).wait_send()

    @pl.loop(1, groups)
    def _(k):
        toward(k).wait_send()

    for j in range(1, n_obs):

        @pl.loop(0, groups)
        def _(k):
            across(k, j).wait_send()


def last_kernel(
    l_ref, w_ref, y_ref, blk_ref, odd_ref, part_ref, back_ref, sum_ref, nw_ref, ny_ref, tprior_ref, trhs_ref,
    oblk_ref, olow_ref, otip_ref, res_ref, sol_ref,
    work, blk, tip, sems,
):
    B = blk_ref.shape[0]
    K = tprior_ref.shape[1]
    copies = [
        pltpu.make_async_copy(l_ref, oblk_ref.at[0], sems.at[0]),
        pltpu.make_async_copy(w_ref, olow_ref.at[0], sems.at[1]),
        pltpu.make_async_copy(odd_ref, olow_ref.at[1], sems.at[2]),
        pltpu.make_async_copy(y_ref.at[pl.ds(B, K)], otip_ref.at[0], sems.at[3]),
    ]
    for copy in copies:
        copy.start()
    next_s = split2(nw_ref[...])
    blk[...] = blk_ref[...] - mm3(next_s, next_s, TN)
    right = mm3(split2(ny_ref[...]), next_s, NN)
    tip[...] = part_ref[:K, :] - right[:K]
    late = [
        pltpu.make_async_copy(blk, oblk_ref.at[1], sems.at[4]),
        pltpu.make_async_copy(tip, otip_ref.at[1], sems.at[5]),
    ]
    for copy in late:
        copy.start()
    res_ref[1:2, :] = part_ref[K : K + 1, :] - right[K : K + 1]
    work[:, :T] = sum_ref[:K, :] + tprior_ref[...] * eye(T)
    work[:, T:] = eye(T)
    factor_tiles([work])
    inv = jnp.where(upper_mask(T).T, work[:, T:], 0.0)
    vec = jnp.concatenate([trhs_ref[...] - sum_ref[K : K + 1, :]] * SUB, axis=0)
    sol = dot(dot(vec, inv, NT), inv, NN)
    sol_ref[...] = sol[0:1, :]
    res_ref[0:1, :] = back_ref[K : K + 1, :] - dot(sol, back_ref[:K, :], NN)[0:1, :]
    for copy in copies + late:
        copy.wait()


def vmem(shape):
    return pltpu.VMEM(shape, jnp.float32)


def local(
    obs_rows, obs_owner, obs_member, prior_diag, lower_coupling, tip_coupling, time_rhs, tip_prior, tip_rhs,
):
    groups, members = lax.axis_size("tm"), lax.axis_size("obs")
    n = groups * members
    B = prior_diag.shape[1]
    K = tip_coupling.shape[1]
    nb = B // T
    width = R * B + T
    count = n * CAP * R
    wide = K + SUB
    sems = [4, groups, groups, groups * members, groups * members, wide // SUB, n, n, wide // SUB, 2 * nb, 2 * nb]
    held = pl.pallas_call(
        main_kernel,
        out_shape=[
            vmem(s)
            for s in (
                (B, B), (B, B), (B + wide, B), (B, B), (B, B), (wide, B), (wide, B), (wide, K), (B, B), (wide, B),
            )
        ],
        in_specs=[VMEM, VMEM, VMEM, VMEM, ANY, ANY, VMEM],
        out_specs=[VMEM] * 10,
        scratch_shapes=[
            vmem(s)
            for s in (
                (B, B), (2, K, B), (groups, CAP, width), (groups, CAP, width), (members, groups, CAP, width),
                (count, B), (count, B), (B, B), (T, 2 * T), (T, 2 * T), (wide, K), (n, SUB, K), (wide, K),
            )
        ]
        + [pltpu.SemaphoreType.DMA((s,)) for s in sems],
        compiler_params=pltpu.CompilerParams(
            vmem_limit_bytes=40 << 20, collective_id=1, has_side_effects=True
        ),
    )(
        obs_rows, obs_owner.reshape(1, -1), obs_member.reshape(1, -1), prior_diag, lower_coupling, tip_coupling,
        time_rhs,
    )
    block, low, tip, result, sol = pl.pallas_call(
        last_kernel,
        out_shape=[
            jax.ShapeDtypeStruct(s, jnp.float32) for s in ((2, B, B), (2, B, B), (2, K, B), (2, B), (1, K))
        ],
        in_specs=[VMEM] * 12,
        out_specs=[ANY, ANY, ANY, VMEM, VMEM],
        scratch_shapes=[vmem((T, 2 * T)), vmem((B, B)), vmem((K, B)), pltpu.SemaphoreType.DMA((6,))],
        compiler_params=pltpu.CompilerParams(vmem_limit_bytes=40 << 20),
    )(*held, tip_prior[None, :], tip_rhs[None, :])
    return block, low, tip, result, sol[0]


def solution(mesh):
    split = ("tm", "obs")
    two, three = P(split, None), P(split, None, None)
    return jax.shard_map(
        local,
        mesh=mesh,
        in_specs=(two, two, two, two, three, three, two, P(), P()),
        out_specs=(three, three, three, two, P()),
        check_vma=False,
    )
```

```python
import jax
import jax.numpy as jnp
from jax import lax
from jax.experimental import pallas as pl
from jax.experimental.pallas import tpu as pltpu
from jax.sharding import PartitionSpec as P

R = 2
CAP = 2
T = 128
PANEL = 16
SUB = 8
HI = lax.Precision.HIGHEST
VMEM = pl.BlockSpec(memory_space=pltpu.VMEM)
HBM = pl.BlockSpec(memory_space=pltpu.HBM)
MESH = pl.DeviceIdType.MESH
NN = (((1,), (0,)), ((), ()))
NT = (((1,), (1,)), ((), ()))
TN = (((0,), (0,)), ((), ()))


def dot(a, b, dims):
    return lax.dot_general(a, b, dims, precision=HI, preferred_element_type=jnp.float32)


def split2(x):
    h = x.astype(jnp.bfloat16)
    return h, (x - h.astype(jnp.float32)).astype(jnp.bfloat16)


def split3(x):
    h = x.astype(jnp.bfloat16)
    rest = x - h.astype(jnp.float32)
    m = rest.astype(jnp.bfloat16)
    return h, m, (rest - m.astype(jnp.float32)).astype(jnp.bfloat16)


def mm3(a, b, dims):
    (ca,), (cb,) = dims[0]
    left = jnp.concatenate([a[0], a[1], a[0]], axis=ca)
    right = jnp.concatenate([b[0], b[0], b[1]], axis=cb)
    return lax.dot_general(left, right, dims, preferred_element_type=jnp.float32)


def panel_gram(rows):
    h, m, l = split3(rows)
    left = jnp.concatenate([part[:, :T] for part in (h, h, m, h, l, m)], axis=0)
    right = jnp.concatenate([h, m, h, l, h, m], axis=0)
    return lax.dot_general(left, right, TN, preferred_element_type=jnp.float32)


def spread(x, i):
    return jnp.broadcast_to(x[i : i + 1, :], x.shape)


def eliminate(rows, base):
    groups = PANEL // SUB
    sub = lax.broadcasted_iota(jnp.int32, (SUB, T), 0)
    lane = lax.broadcasted_iota(jnp.int32, (SUB, T), 1)
    left = [rows[SUB * g : SUB * (g + 1), :T] for g in range(groups)]
    right = [rows[SUB * g : SUB * (g + 1), T:] for g in range(groups)]
    cols = [
        [
            jnp.broadcast_to(jnp.sum(jnp.where(lane == base + j, x, 0.0), axis=1, keepdims=True), (SUB, T))
            for x in left
        ]
        for j in range(PANEL)
    ]
    scale = [jnp.zeros((SUB, T), jnp.float32) for _ in range(groups)]
    for i in range(0, PANEL, 2):
        first, s = i // SUB, i % SUB
        a = spread(cols[i][first], s)
        b = spread(cols[i + 1][first], s)
        c = spread(cols[i + 1][first], s + 1)
        det = a * c - b * b
        inv_det, inv_a = 1.0 / det, 1.0 / a
        scale[first] = jnp.where(
            sub == s, lax.rsqrt(a), jnp.where(sub == s + 1, lax.rsqrt(det * inv_a), scale[first])
        )
        l1, l2 = spread(left[first], s), spread(left[first], s + 1)
        r1, r2 = spread(right[first], s), spread(right[first], s + 1)
        heads = {j: (spread(cols[j][first], s), spread(cols[j][first], s + 1)) for j in range(i + 2, PANEL)}
        for g in range(first, groups):
            ci, cj = cols[i][g], cols[i + 1][g]
            n1, n2 = c * ci - b * cj, a * cj - b * ci
            if g == first:
                n1, n2 = jnp.where(sub > s + 1, n1, 0.0), jnp.where(sub > s + 1, n2, 0.0)
            m1, m2 = n1 * inv_det, n2 * inv_det
            if g > first or s + 2 < SUB:
                for j in range(i + 2, PANEL):
                    cols[j][g] = cols[j][g] - m1 * heads[j][0] - m2 * heads[j][1]
            if g == first:
                m1 = jnp.where(sub == s + 1, b * inv_a, m1)
            left[g] = left[g] - m1 * l1 - m2 * l2
            right[g] = right[g] - m1 * r1 - m2 * r2
    return jnp.concatenate(
        [jnp.concatenate([left[g] * scale[g], right[g] * scale[g]], axis=1) for g in range(groups)], axis=0
    )


def factor_tiles(works, jobs=()):
    steps = T // PANEL
    for p in range(steps):
        base = p * PANEL
        below = base + PANEL
        done = [eliminate(work[base:below, :], base) for work in works]
        for work, rows in zip(works, done):
            work[base:below, :] = rows
        for job in jobs[p * len(jobs) // steps : (p + 1) * len(jobs) // steps]:
            job()
        if below < T:
            for work, rows in zip(works, done):
                work[below:, :] = work[below:, :] - panel_gram(rows)[below:, :]


def eye(n):
    return (
        lax.broadcasted_iota(jnp.int32, (n, n), 0) == lax.broadcasted_iota(jnp.int32, (n, n), 1)
    ).astype(jnp.float32)


def upper_mask(n):
    return lax.broadcasted_iota(jnp.int32, (n, n), 0) <= lax.broadcasted_iota(jnp.int32, (n, n), 1)


def pack(rows_ref, owner_ref, member_ref, out_ref):
    groups = out_ref.shape[0]
    blocks, width = rows_ref.shape
    owners = owner_ref[...]
    named = (lax.broadcasted_iota(jnp.int32, (groups, blocks), 0) == owners).astype(jnp.float32)
    before = lax.broadcasted_iota(jnp.int32, (blocks, blocks), 0) < lax.broadcasted_iota(
        jnp.int32, (blocks, blocks), 1
    )
    rank = jnp.sum(dot(named, before.astype(jnp.float32), NN) * named, axis=0, keepdims=True)
    slot = owners.astype(jnp.float32) * CAP + rank
    spots = lax.broadcasted_iota(jnp.int32, (groups * CAP, blocks), 0).astype(jnp.float32)
    pick = (spots == slot).astype(jnp.float32)
    rows = dot(pick, rows_ref[...], NN)
    tag = jnp.sum(pick * (member_ref[...].astype(jnp.float32) + 1.0), axis=1, keepdims=True)
    tags = jnp.broadcast_to(tag, (groups * CAP, T))
    for g in range(groups):
        out_ref[g, :, :width] = rows[g * CAP : (g + 1) * CAP, :]
        out_ref[g, :, width:] = tags[g * CAP : (g + 1) * CAP, :]


def main_kernel(
    rows_in, owner_in, member_in, prior_in, lower_in, tip_in, rhs_in, tprior_in, trhs_in,
    l_ref, w_ref, y_ref, blk_ref, odd_ref, part_ref, nw_ref, ny_ref, res_ref, sol_ref,
    rows_ref, owner_ref, member_ref, prior_ref, tip, rhs_ref, tprior_ref, trhs_ref, outgoing,
    stage, landed, even_rows, odd_rows, gram, work, work_k, flat, parts, total, base_ref, back_ref,
    local_sem, send_a, recv_a, send_b, recv_b, send_c, recv_c, send_d, recv_d, send_e, recv_e,
):
    groups, n_obs = lax.axis_size("tm"), lax.axis_size("obs")
    n = groups * n_obs
    t, o = lax.axis_index("tm"), lax.axis_index("obs")
    me = t * n_obs + o
    B = prior_ref.shape[1]
    K = tip.shape[1]
    nb = B // T
    chunks = (K + SUB) // SUB
    count = n * CAP * R
    early = count <= T

    def wrap(i, size):
        return jnp.where(i >= size, i - size, i)

    def remote(src, dst, send, recv, where):
        return pltpu.make_async_remote_copy(
            src_ref=src, dst_ref=dst, send_sem=send, recv_sem=recv, device_id=where, device_id_type=MESH
        )

    def toward(k):
        peer = wrap(t + k, groups)
        return remote(outgoing.at[peer], stage.at[k], send_a.at[k], recv_a.at[k], (peer, o))

    def across(k, j):
        slot = k * n_obs + j
        return remote(stage.at[k], landed.at[j, k], send_b.at[slot], recv_b.at[slot], (t, wrap(o + j, n_obs)))

    owners = [i * n // chunks for i in range(chunks)]
    mine = (me * chunks + n - 1) // n
    reducing = jnp.logical_and(mine < chunks, mine * n // chunks == me)

    def rows_of(i):
        return pl.ds(pl.multiple_of(i * SUB, SUB), SUB)

    def each_owner(act):
        for i, owner in enumerate(owners):

            @pl.when(me != owner)
            def _():
                act(i, (owner // n_obs, owner % n_obs))

    def scatter(i, where):
        return remote(flat.at[pl.ds(i * SUB, SUB)], parts.at[me], send_c.at[i], recv_c.at[me], where)

    def collect(i, where):
        rows = pl.ds(i * SUB, SUB)
        return remote(total.at[rows], total.at[rows], send_d.at[0], recv_d.at[i], where)

    def each_other(act):
        @pl.loop(0, groups)
        def _(i):
            for j in range(n_obs):
                k = i * n_obs + j

                @pl.when(k != me)
                def _():
                    act(k, (i, j))

    def arrive(k, where):
        return remote(flat.at[pl.ds(0, SUB)], parts.at[k], send_c.at[0], recv_c.at[k], where)

    def gather(k, where):
        rows = rows_of(mine)
        return remote(total.at[rows], total.at[rows], send_d.at[k], recv_d.at[mine], where)

    before = (jnp.where(o > 0, t, wrap(t + groups - 1, groups)), wrap(o + n_obs - 1, n_obs))

    def shift(b):
        rows, lanes = pl.ds(b * T, T), pl.ds(b * T, T)
        return (
            remote(w_ref.at[rows], nw_ref.at[rows], send_e.at[2 * b], recv_e.at[2 * b], before),
            remote(
                y_ref.at[pl.ds(B, K + SUB), lanes], ny_ref.at[:, lanes],
                send_e.at[2 * b + 1], recv_e.at[2 * b + 1], before,
            ),
        )

    barrier = pltpu.get_barrier_semaphore()
    pairs = [
        (rows_in, rows_ref), (owner_in, owner_ref), (member_in, member_ref), (prior_in, prior_ref),
        (rhs_in, rhs_ref), (tprior_in, tprior_ref), (trhs_in, trhs_ref), (tip_in, tip), (lower_in.at[0], w_ref), (lower_in.at[1], y_ref.at[pl.ds(0, B)]),
    ]
    loads = [pltpu.make_async_copy(src, dst, local_sem.at[1 + i]) for i, (src, dst) in enumerate(pairs)]
    for load in loads:
        load.start()

    @pl.loop(1, groups)
    def _(k):
        pl.semaphore_signal(barrier, inc=1, device_id=(wrap(t + k, groups), o), device_id_type=MESH)

    for j in range(1, n_obs):
        pl.semaphore_signal(barrier, inc=1, device_id=(t, wrap(o + j, n_obs)), device_id_type=MESH)
    for load in loads[:3]:
        load.wait()
    pack(rows_ref, owner_ref, member_ref, outgoing)
    pl.semaphore_wait(barrier, groups + n_obs - 2)

    @pl.loop(1, groups)
    def _(k):
        toward(k).start()

    own = pltpu.make_async_copy(outgoing.at[t], stage.at[0], local_sem.at[0])
    own.start()
    own.wait()
    for j in range(1, n_obs):
        across(0, j).start()

    @pl.loop(1, groups)
    def _(k):
        toward(k).wait_recv()
        for j in range(1, n_obs):
            across(k, j).start()

    for load in loads[3:]:
        load.wait()

    @pl.when(me == 0)
    def _():
        w_ref[...] = jnp.zeros((B, B), jnp.float32)

    y_ref[B : B + K, :] = tip[0]
    y_ref[B + K :, :] = jnp.concatenate([rhs_ref[0:1, :], jnp.zeros((SUB - 1, B), jnp.float32)], axis=0)
    part_ref[:K, :] = tip[1]
    part_ref[K:, :] = jnp.concatenate([rhs_ref[1:2, :], jnp.zeros((SUB - 1, B), jnp.float32)], axis=0)
    root = lax.rsqrt(prior_ref[0:1, :])
    scaled = y_ref[B:, :] * root
    both = dot(tip[0], tip[0], NT) + dot(tip[1], tip[1], NT)
    if early:
        inner = dot(scaled, scaled[:K], NT)
        base_ref[:K, :] = both - inner[:K]
        base_ref[K:, :] = inner[K:]
    else:
        base_ref[:K, :] = both
        base_ref[K:, :] = jnp.zeros((SUB, K), jnp.float32)
    for b in range(nb - 1):
        l_ref[b * T : (b + 1) * T, (b + 1) * T :] = jnp.zeros((T, B - (b + 1) * T), jnp.float32)

    @pl.when(me == n - 1)
    def _():
        nw_ref[...] = jnp.zeros((B, B), jnp.float32)
        ny_ref[...] = jnp.zeros((K + SUB, B), jnp.float32)

    @pl.loop(0, groups)
    def _(k):
        for j in range(1, n_obs):
            across(k, j).wait_recv()

    even = (2 * o + 1).astype(jnp.float32)
    odd = even + 1.0
    each = SUB // CAP
    pieces = [(j, k) for j in range(n_obs) for k in range(groups)]
    for q in range(0, n, each):
        block = jnp.concatenate([landed[j, k] if j else stage[k] for j, k in pieces[q : q + each]], axis=0)
        tag = block[:, R * B :]
        for r in range(R):
            at = r * n * CAP + q * CAP
            for c in range(nb):
                x = block[:, r * B + c * T : r * B + (c + 1) * T]
                even_rows[at : at + SUB, c * T : (c + 1) * T] = jnp.where(tag == even, x, 0.0)
                odd_rows[at : at + SUB, c * T : (c + 1) * T] = jnp.where(tag == odd, x, 0.0)
    chosen = even_rows[...]
    gram[...] = dot(chosen, chosen, TN) + prior_ref[0:1, :] * eye(B)
    if early:
        weighed = chosen * root
        if count < T:
            weighed = jnp.concatenate([weighed, jnp.zeros((T - count, B), jnp.float32)], axis=0)
        work_k[:, :T] = dot(weighed, weighed, NT) + eye(T)
        work_k[:, T:] = eye(T)
        crossed = dot(scaled, weighed, NT)

    def terms(seen, sign):
        flat[:K, :] = base_ref[:K, :] + sign * seen[:K]
        flat[K:, :] = base_ref[K:, :] - sign * seen[K:]
        each_owner(lambda i, where: scatter(i, where).start())

    def combine():
        @pl.when(reducing)
        def _():
            parts[me] = flat[rows_of(mine)]
            each_other(lambda k, where: arrive(k, where).wait_recv())
            if n <= 64:
                value = parts[0]
                for k in range(1, n):
                    value = value + parts[k]
            else:
                value = lax.fori_loop(1, n, lambda k, acc: acc + parts[k], parts[0])
            total[rows_of(mine)] = value
            each_other(lambda k, where: gather(k, where).start())

    def tip_system():
        each_owner(lambda i, where: collect(i, where).wait_recv())
        work_k[:, :T] = total[:K, :] + tprior_ref[...] * eye(T)
        work_k[:, T:] = eye(T)

    upper = upper_mask(T)

    def odd_gram(c):
        def job():
            at = slice(c * T, (c + 1) * T)
            wide = (lax.broadcasted_iota(jnp.int32, (T, B), 0) + c * T) == lax.broadcasted_iota(jnp.int32, (T, B), 1)
            blk_ref[at, :] = dot(odd_rows[:, at], odd_rows[...], TN) + jnp.where(wide, prior_ref[1:2, :], 0.0)

        return job

    def solve_jobs(b, inv_s):
        at = slice(b * T, (b + 1) * T)

        def fill():
            w_ref[at, :] = mm3(inv_s, split2(w_ref[at, :]), NN)

        def side(rows):
            def job():
                y_ref[rows, at] = mm3(split2(y_ref[rows, at]), inv_s, NT)

            return job

        def send():
            @pl.when(me > 0)
            def _():
                for copy in shift(b):
                    copy.start()

        return [fill, side(slice(B, None)), send, side(slice(0, B))]

    def update_jobs(b, rest_s):
        at, after = slice(b * T, (b + 1) * T), slice((b + 1) * T, None)

        def fill():
            w_ref[after, :] = w_ref[after, :] - mm3(rest_s, split2(w_ref[at, :]), TN)

        def side(rows):
            def job():
                y_ref[rows, after] = y_ref[rows, after] - mm3(split2(y_ref[rows, at]), rest_s, NN)

            return job

        return [fill, side(slice(B, None)), side(slice(0, B))]

    def product_jobs(b):
        at = slice(b * T, (b + 1) * T)

        def square(c):
            def job():
                rows = slice(c * T, (c + 1) * T)
                blk_ref[rows, :] = blk_ref[rows, :] - mm3(split2(y_ref[rows, at]), split2(y_ref[:B, at]), NT)

            return job

        def link(c):
            def job():
                rows = slice(c * T, (c + 1) * T)
                value = mm3(split2(y_ref[rows, at]), split2(w_ref[at, :]), NN)
                odd_ref[rows, :] = odd_ref[rows, :] - value if b else -value

            return job

        def side():
            part_ref[...] = part_ref[...] - mm3(split2(y_ref[B:, at]), split2(y_ref[:B, at]), NT)

        return [side] + [square(c) for c in range(nb)] + [link(c) for c in range(nb)]

    def next_jobs(b):
        at = slice(b * T, (b + 1) * T)

        def wait():
            @pl.when(me < n - 1)
            def _():
                for copy in shift(b):
                    copy.wait_recv()

        def square(c):
            def job():
                rows = slice(c * T, (c + 1) * T)
                blk_ref[rows, :] = blk_ref[rows, :] - mm3(split2(nw_ref[at, rows]), split2(nw_ref[at, :]), TN)

            return job

        def side():
            part_ref[...] = part_ref[...] - mm3(split2(ny_ref[:, at]), split2(nw_ref[at, :]), NN)

        return [wait, side] + [square(c) for c in range(nb)]

    jobs = [odd_gram(c) for c in range(nb)]
    inverse = []
    for b in range(nb):
        lo, hi = b * T, (b + 1) * T
        last = b + 1 == nb
        work[:, :T] = gram[lo:hi, lo:hi]
        work[:, T:] = eye(T)
        works = [work]
        if b == 0 and early:
            works = [work, work_k]
        elif b == 1 and early and not last:
            at = 3 * len(jobs) // 4
            jobs = jobs[:at] + [combine] + jobs[at:]
        factor_tiles(works, jobs)
        if b == 0 and early:
            side = dot(crossed, jnp.where(upper.T, work_k[:, T:], 0.0), NT)
            terms(dot(side, side[:K], NT), 1.0)
        inv_b = jnp.where(upper.T, work[:, T:], 0.0)
        inv_s = split2(inv_b)
        inverse.append(inv_s)
        l_ref[lo:hi, lo:hi] = jnp.where(upper, work[:, :T], 0.0).T
        jobs = solve_jobs(b, inv_s)
        if last:
            for job in jobs:
                job()
            jobs = []
        else:
            rest = dot(inv_b, gram[lo:hi, hi:], NN)
            gram[hi:, hi:] = gram[hi:, hi:] - dot(rest, rest, TN)
            l_ref[hi:, lo:hi] = rest.T
            jobs = jobs + update_jobs(b, split2(rest))
        jobs = jobs + product_jobs(b)
        if b:
            jobs = jobs + next_jobs(b - 1)
    if not early:
        side = y_ref[B:, :]
        terms(dot(side, side[:K], NT), -1.0)
    if not early or nb < 2:
        combine()

    def back_job(b):
        def job():
            at, after = slice(b * T, (b + 1) * T), slice((b + 1) * T, None)
            value = y_ref[B:, at]
            if b + 1 < nb:
                value = value - mm3(split2(back_ref[:, after]), split2(l_ref[after, at]), NN)
            back_ref[:, at] = mm3(split2(value), inverse[b], NN)

        return job

    tip_system()
    factor_tiles([work_k], [back_job(b) for b in reversed(range(nb))] + jobs)
    inv = jnp.where(upper.T, work_k[:, T:], 0.0)
    vec = jnp.concatenate([trhs_ref[...] - total[K : K + 1, :]] * SUB, axis=0)
    sol = dot(dot(vec, inv, NT), inv, NN)
    sol_ref[...] = sol
    res_ref[...] = back_ref[K:, :] - dot(sol, back_ref[:K, :], NN)

    each_owner(lambda i, where: scatter(i, where).wait_send())

    @pl.when(reducing)
    def _():
        each_other(lambda k, where: gather(k, where).wait_send())

    @pl.loop(1, groups)
    def _(k):
        toward(k).wait_send()

    @pl.loop(0, groups)
    def _(k):
        for j in range(1, n_obs):
            across(k, j).wait_send()

    @pl.when(me > 0)
    def _():
        for b in range(nb):
            for copy in shift(b):
                copy.wait_send()

    @pl.when(me < n - 1)
    def _():
        for copy in shift(nb - 1):
            copy.wait_recv()


def last_kernel(
    l_ref, w_ref, y_ref, blk_ref, odd_ref, part_ref, nw_ref, ny_ref, even_ref, tip_ref,
    oblk_ref, olow_ref, otip_ref, res_ref, sol_ref,
    blk, tip, sems,
):
    B = blk_ref.shape[0]
    K = tip_ref.shape[1]
    copies = [
        pltpu.make_async_copy(l_ref, oblk_ref.at[0], sems.at[0]),
        pltpu.make_async_copy(w_ref, olow_ref.at[0], sems.at[1]),
        pltpu.make_async_copy(odd_ref, olow_ref.at[1], sems.at[2]),
        pltpu.make_async_copy(y_ref.at[pl.ds(B, K)], otip_ref.at[0], sems.at[3]),
    ]
    for copy in copies:
        copy.start()
    next_s = split2(nw_ref[B - T :, :])
    blk[...] = blk_ref[...] - mm3(next_s, next_s, TN)
    square = pltpu.make_async_copy(blk, oblk_ref.at[1], sems.at[4])
    square.start()
    right = part_ref[...] - mm3(split2(ny_ref[:, B - T :]), next_s, NN)
    tip[...] = right[:K]
    side = pltpu.make_async_copy(tip, otip_ref.at[1], sems.at[5])
    side.start()
    res_ref[0:1, :] = even_ref[0:1, :]
    res_ref[1:2, :] = right[K : K + 1]
    sol_ref[...] = tip_ref[0:1, :]
    for copy in copies + [square, side]:
        copy.wait()


def vmem(shape):
    return pltpu.VMEM(shape, jnp.float32)


def local(
    obs_rows, obs_owner, obs_member, prior_diag, lower_coupling, tip_coupling, time_rhs, tip_prior, tip_rhs,
):
    groups, members = lax.axis_size("tm"), lax.axis_size("obs")
    n = groups * members
    B = prior_diag.shape[1]
    K = tip_coupling.shape[1]
    nb = B // T
    width = R * B + T
    count = n * CAP * R
    wide = K + SUB
    sems = [11, groups, groups, groups * members, groups * members, wide // SUB, n, n, wide // SUB, 2 * nb, 2 * nb]
    held = pl.pallas_call(
        main_kernel,
        out_shape=[
            vmem(s)
            for s in (
                (B, B), (B, B), (B + wide, B), (B, B), (B, B), (wide, B), (B, B), (wide, B), (SUB, B), (SUB, K),
            )
        ],
        in_specs=[HBM] * 9,
        out_specs=[VMEM] * 10,
        scratch_shapes=[
            vmem(obs_rows.shape),
            pltpu.VMEM((1, obs_owner.size), jnp.int32),
            pltpu.VMEM((1, obs_owner.size), jnp.int32),
        ]
        + [
            vmem(s)
            for s in (
                (2, B), (2, K, B), (2, B), (1, K), (1, K), (groups, CAP, width), (groups, CAP, width), (members, groups, CAP, width),
                (count, B), (count, B), (B, B), (T, 2 * T), (T, 2 * T), (wide, K), (n, SUB, K), (wide, K), (wide, K),
                (wide, B),
            )
        ]
        + [pltpu.SemaphoreType.DMA((s,)) for s in sems],
        compiler_params=pltpu.CompilerParams(
            vmem_limit_bytes=40 << 20, collective_id=1, has_side_effects=True
        ),
    )(
        *(
            pltpu.with_memory_space_constraint(x, pltpu.HBM)
            for x in (
                obs_rows, obs_owner.reshape(1, -1), obs_member.reshape(1, -1), prior_diag, lower_coupling,
                tip_coupling, time_rhs, tip_prior[None, :], tip_rhs[None, :],
            )
        )
    )
    block, low, tip, result, sol = pl.pallas_call(
        last_kernel,
        out_shape=[
            jax.ShapeDtypeStruct(s, jnp.float32) for s in ((2, B, B), (2, B, B), (2, K, B), (2, B), (1, K))
        ],
        in_specs=[VMEM] * 10,
        out_specs=[HBM, HBM, HBM, VMEM, VMEM],
        scratch_shapes=[vmem((B, B)), vmem((K, B)), pltpu.SemaphoreType.DMA((6,))],
        compiler_params=pltpu.CompilerParams(vmem_limit_bytes=40 << 20),
    )(*held)
    return block, low, tip, result, sol[0]


def solution(mesh):
    split = ("tm", "obs")
    two, three = P(split, None), P(split, None, None)
    return jax.shard_map(
        local,
        mesh=mesh,
        in_specs=(two, two, two, two, three, three, two, P(), P()),
        out_specs=(three, three, three, two, P()),
        check_vma=False,
    )
```

```python
import jax
import jax.numpy as jnp
from jax import lax
from jax.experimental import pallas as pl
from jax.experimental.pallas import tpu as pltpu
from jax.sharding import PartitionSpec as P

R = 2
CAP = 2
T = 128
PANEL = 16
SUB = 8
HI = lax.Precision.HIGHEST
VMEM = pl.BlockSpec(memory_space=pltpu.VMEM)
HBM = pl.BlockSpec(memory_space=pltpu.HBM)
MESH = pl.DeviceIdType.MESH
NN = (((1,), (0,)), ((), ()))
NT = (((1,), (1,)), ((), ()))
TN = (((0,), (0,)), ((), ()))


def dot(a, b, dims):
    return lax.dot_general(a, b, dims, precision=HI, preferred_element_type=jnp.float32)


def split2(x):
    h = x.astype(jnp.bfloat16)
    return h, (x - h.astype(jnp.float32)).astype(jnp.bfloat16)


def split3(x):
    h = x.astype(jnp.bfloat16)
    rest = x - h.astype(jnp.float32)
    m = rest.astype(jnp.bfloat16)
    return h, m, (rest - m.astype(jnp.float32)).astype(jnp.bfloat16)


def mm3(a, b, dims):
    (ca,), (cb,) = dims[0]
    left = jnp.concatenate([a[0], a[1], a[0]], axis=ca)
    right = jnp.concatenate([b[0], b[0], b[1]], axis=cb)
    return lax.dot_general(left, right, dims, preferred_element_type=jnp.float32)


def panel_gram(rows):
    h, m, l = split3(rows)
    left = jnp.concatenate([part[:, :T] for part in (h, h, m, h, l, m)], axis=0)
    right = jnp.concatenate([h, m, h, l, h, m], axis=0)
    return lax.dot_general(left, right, TN, preferred_element_type=jnp.float32)


def spread(x, i):
    return jnp.broadcast_to(x[i : i + 1, :], x.shape)


def eliminate(rows, base):
    groups = PANEL // SUB
    sub = lax.broadcasted_iota(jnp.int32, (SUB, T), 0)
    lane = lax.broadcasted_iota(jnp.int32, (SUB, T), 1)
    left = [rows[SUB * g : SUB * (g + 1), :T] for g in range(groups)]
    right = [rows[SUB * g : SUB * (g + 1), T:] for g in range(groups)]
    cols = [
        [
            jnp.broadcast_to(jnp.sum(jnp.where(lane == base + j, x, 0.0), axis=1, keepdims=True), (SUB, T))
            for x in left
        ]
        for j in range(PANEL)
    ]
    scale = [jnp.zeros((SUB, T), jnp.float32) for _ in range(groups)]
    for i in range(0, PANEL, 2):
        first, s = i // SUB, i % SUB
        a = spread(cols[i][first], s)
        b = spread(cols[i + 1][first], s)
        c = spread(cols[i + 1][first], s + 1)
        det = a * c - b * b
        inv_det, inv_a = 1.0 / det, 1.0 / a
        scale[first] = jnp.where(
            sub == s, lax.rsqrt(a), jnp.where(sub == s + 1, lax.rsqrt(det * inv_a), scale[first])
        )
        l1, l2 = spread(left[first], s), spread(left[first], s + 1)
        r1, r2 = spread(right[first], s), spread(right[first], s + 1)
        heads = {j: (spread(cols[j][first], s), spread(cols[j][first], s + 1)) for j in range(i + 2, PANEL)}
        for g in range(first, groups):
            ci, cj = cols[i][g], cols[i + 1][g]
            n1, n2 = c * ci - b * cj, a * cj - b * ci
            if g == first:
                n1, n2 = jnp.where(sub > s + 1, n1, 0.0), jnp.where(sub > s + 1, n2, 0.0)
            m1, m2 = n1 * inv_det, n2 * inv_det
            if g > first or s + 2 < SUB:
                for j in range(i + 2, PANEL):
                    cols[j][g] = cols[j][g] - m1 * heads[j][0] - m2 * heads[j][1]
            if g == first:
                m1 = jnp.where(sub == s + 1, b * inv_a, m1)
            left[g] = left[g] - m1 * l1 - m2 * l2
            right[g] = right[g] - m1 * r1 - m2 * r2
    return jnp.concatenate(
        [jnp.concatenate([left[g] * scale[g], right[g] * scale[g]], axis=1) for g in range(groups)], axis=0
    )


def factor_tiles(works, jobs=()):
    steps = T // PANEL
    for p in range(steps):
        base = p * PANEL
        below = base + PANEL
        done = [eliminate(work[base:below, :], base) for work in works]
        for work, rows in zip(works, done):
            work[base:below, :] = rows
        for job in jobs[p * len(jobs) // steps : (p + 1) * len(jobs) // steps]:
            job()
        if below < T:
            for work, rows in zip(works, done):
                work[below:, :] = work[below:, :] - panel_gram(rows)[below:, :]


def eye(n):
    return (
        lax.broadcasted_iota(jnp.int32, (n, n), 0) == lax.broadcasted_iota(jnp.int32, (n, n), 1)
    ).astype(jnp.float32)


def upper_mask(n):
    return lax.broadcasted_iota(jnp.int32, (n, n), 0) <= lax.broadcasted_iota(jnp.int32, (n, n), 1)


def pack(rows_ref, owner_ref, member_ref, out_ref):
    groups = out_ref.shape[0]
    blocks, width = rows_ref.shape
    owners = owner_ref[...]
    down = lax.broadcasted_iota(jnp.int32, (blocks, blocks), 0)
    along = lax.broadcasted_iota(jnp.int32, (blocks, blocks), 1)
    wide = jnp.broadcast_to(owners.astype(jnp.float32), (blocks, blocks))
    column = jnp.sum(jnp.where(down == along, wide, 0.0), axis=1, keepdims=True)
    same = jnp.logical_and(column == wide, down < along)
    rank = jnp.sum(same.astype(jnp.int32), axis=0, keepdims=True)
    slot = owners * CAP + rank
    pick = (lax.broadcasted_iota(jnp.int32, (groups * CAP, blocks), 0) == slot).astype(jnp.float32)
    parts = jnp.concatenate([part.astype(jnp.float32) for part in split3(rows_ref[...])], axis=0)
    rows = lax.dot_general(
        jnp.concatenate([pick] * 3, axis=1).astype(jnp.bfloat16), parts.astype(jnp.bfloat16), NN,
        preferred_element_type=jnp.float32,
    )
    tag = jnp.sum(pick * (member_ref[...].astype(jnp.float32) + 1.0), axis=1, keepdims=True)
    tags = jnp.broadcast_to(tag, (groups * CAP, T))
    for g in range(groups):
        out_ref[g, :, :width] = rows[g * CAP : (g + 1) * CAP, :]
        out_ref[g, :, width:] = tags[g * CAP : (g + 1) * CAP, :]


def main_kernel(
    rows_in, owner_in, member_in, prior_in, lower_in, tip_in, rhs_in, tprior_in, trhs_in,
    l_ref, w_ref, y_ref, blk_ref, odd_ref, part_ref, nw_ref, ny_ref, res_ref, sol_ref,
    rows_ref, owner_ref, member_ref, prior_ref, tip, rhs_ref, tprior_ref, trhs_ref, outgoing,
    stage, landed, even_rows, odd_rows, gram, work, work_k, flat, parts, total, base_ref, back_ref,
    local_sem, send_a, recv_a, send_b, recv_b, send_c, recv_c, send_d, recv_d, send_e, recv_e,
):
    groups, n_obs = lax.axis_size("tm"), lax.axis_size("obs")
    n = groups * n_obs
    t, o = lax.axis_index("tm"), lax.axis_index("obs")
    me = t * n_obs + o
    B = prior_ref.shape[1]
    K = tip.shape[1]
    nb = B // T
    chunks = (K + SUB) // SUB
    count = n * CAP * R
    early = count <= T

    def wrap(i, size):
        return jnp.where(i >= size, i - size, i)

    def remote(src, dst, send, recv, where):
        return pltpu.make_async_remote_copy(
            src_ref=src, dst_ref=dst, send_sem=send, recv_sem=recv, device_id=where, device_id_type=MESH
        )

    def whole(ref, sem):
        pltpu.make_async_copy(ref, ref, sem.at[0]).wait()

    def toward(k):
        peer = wrap(t + k, groups)
        return remote(outgoing.at[peer], stage.at[k], send_a.at[0], recv_a.at[k], (peer, o))

    def across(k, j, passed=True):
        source = stage.at[k] if passed else outgoing.at[t]
        return remote(source, landed.at[j, k], send_b.at[0], recv_b.at[0], (t, wrap(o + j, n_obs)))

    owners = [i * n // chunks for i in range(chunks)]
    mine = (me * chunks + n - 1) // n
    reducing = jnp.logical_and(mine < chunks, mine * n // chunks == me)

    def rows_of(i):
        return pl.ds(pl.multiple_of(i * SUB, SUB), SUB)

    def each_owner(act):
        for i, owner in enumerate(owners):

            @pl.when(me != owner)
            def _():
                act(i, (owner // n_obs, owner % n_obs))

    def scatter(i, where):
        return remote(flat.at[pl.ds(i * SUB, SUB)], parts.at[me], send_c.at[0], recv_c.at[0], where)

    def owned(ref, sem):
        @pl.when(reducing)
        def _():
            whole(ref.at[pl.ds(0, (chunks - 1) * SUB)], sem)

        @pl.when(jnp.logical_not(reducing))
        def _():
            whole(ref, sem)

    def each_other(act):
        @pl.loop(0, groups)
        def _(i):
            for j in range(n_obs):
                k = i * n_obs + j

                @pl.when(k != me)
                def _():
                    act(k, (i, j))

    def gather(k, where):
        rows = rows_of(mine)
        return remote(total.at[rows], total.at[rows], send_d.at[0], recv_d.at[0], where)

    before = (jnp.where(o > 0, t, wrap(t + groups - 1, groups)), wrap(o + n_obs - 1, n_obs))

    def shift(b):
        rows, lanes = pl.ds(b * T, T), pl.ds(b * T, T)
        return (
            remote(w_ref.at[rows], nw_ref.at[rows], send_e.at[2 * b], recv_e.at[2 * b], before),
            remote(
                y_ref.at[pl.ds(B, K + SUB), lanes], ny_ref.at[:, lanes],
                send_e.at[2 * b + 1], recv_e.at[2 * b + 1], before,
            ),
        )

    barrier = pltpu.get_barrier_semaphore()
    pairs = [
        (rows_in, rows_ref), (owner_in, owner_ref), (member_in, member_ref), (prior_in, prior_ref),
        (rhs_in, rhs_ref), (tprior_in, tprior_ref), (trhs_in, trhs_ref), (tip_in, tip), (lower_in.at[0], w_ref), (lower_in.at[1], y_ref.at[pl.ds(0, B)]),
    ]
    loads = [pltpu.make_async_copy(src, dst, local_sem.at[i]) for i, (src, dst) in enumerate(pairs)]
    for load in loads:
        load.start()

    @pl.loop(1, groups)
    def _(k):
        pl.semaphore_signal(barrier, inc=1, device_id=(wrap(t + k, groups), o), device_id_type=MESH)

    for j in range(1, n_obs):
        pl.semaphore_signal(barrier, inc=1, device_id=(t, wrap(o + j, n_obs)), device_id_type=MESH)
    for load in loads[:3]:
        load.wait()
    pack(rows_ref, owner_ref, member_ref, outgoing)
    pl.semaphore_wait(barrier, groups + n_obs - 2)

    @pl.loop(1, groups)
    def _(k):
        toward(k).start()

    for j in range(1, n_obs):
        across(0, j, False).start()

    @pl.loop(1, groups)
    def _(k):
        toward(k).wait_recv()
        for j in range(1, n_obs):
            across(k, j).start()

    for load in loads[3:]:
        load.wait()

    @pl.when(me == 0)
    def _():
        w_ref[...] = jnp.zeros((B, B), jnp.float32)

    y_ref[B : B + K, :] = tip[0]
    y_ref[B + K :, :] = jnp.concatenate([rhs_ref[0:1, :], jnp.zeros((SUB - 1, B), jnp.float32)], axis=0)
    part_ref[:K, :] = tip[1]
    part_ref[K:, :] = jnp.concatenate([rhs_ref[1:2, :], jnp.zeros((SUB - 1, B), jnp.float32)], axis=0)
    root = lax.rsqrt(prior_ref[0:1, :])
    scaled = y_ref[B:, :] * root
    both = dot(tip[0], tip[0], NT) + dot(tip[1], tip[1], NT)
    if early:
        inner = dot(scaled, scaled[:K], NT)
        base_ref[:K, :] = both - inner[:K]
        base_ref[K:, :] = inner[K:]
    else:
        base_ref[:K, :] = both
        base_ref[K:, :] = jnp.zeros((SUB, K), jnp.float32)
    for b in range(nb - 1):
        l_ref[b * T : (b + 1) * T, (b + 1) * T :] = jnp.zeros((T, B - (b + 1) * T), jnp.float32)

    @pl.when(me == n - 1)
    def _():
        nw_ref[...] = jnp.zeros((B, B), jnp.float32)
        ny_ref[...] = jnp.zeros((K + SUB, B), jnp.float32)

    whole(landed.at[pl.ds(1, n_obs - 1)], recv_b)

    even = (2 * o + 1).astype(jnp.float32)
    odd = even + 1.0
    each = SUB // CAP
    pieces = [(j, k) for j in range(n_obs) for k in range(groups)]
    for q in range(0, n, each):
        block = jnp.concatenate([landed[j, k] if j else stage[k] if k else outgoing[t] for j, k in pieces[q : q + each]], axis=0)
        tag = block[:, R * B :]
        for r in range(R):
            at = r * n * CAP + q * CAP
            for c in range(nb):
                x = block[:, r * B + c * T : r * B + (c + 1) * T]
                even_rows[at : at + SUB, c * T : (c + 1) * T] = jnp.where(tag == even, x, 0.0)
                odd_rows[at : at + SUB, c * T : (c + 1) * T] = jnp.where(tag == odd, x, 0.0)
    chosen = even_rows[...]
    gram[:T, :T] = dot(even_rows[:, :T], even_rows[:, :T], TN) + prior_ref[0:1, :T] * eye(T)
    if early:
        weighed = chosen * root
        if count < T:
            weighed = jnp.concatenate([weighed, jnp.zeros((T - count, B), jnp.float32)], axis=0)
        work_k[:, :T] = dot(weighed, weighed, NT) + eye(T)
        work_k[:, T:] = eye(T)
        crossed = dot(scaled, weighed, NT)

    def even_gram(c):
        def job():
            at, to = slice(c * T, (c + 1) * T), slice(c * T if c else T, None)
            value = dot(even_rows[:, at], even_rows[:, to], TN)
            if c:
                wide = lax.broadcasted_iota(jnp.int32, value.shape, 0) == lax.broadcasted_iota(
                    jnp.int32, value.shape, 1
                )
                value = value + jnp.where(wide, prior_ref[0:1, to], 0.0)
            gram[at, to] = value

        return job

    def terms(seen, sign):
        flat[:K, :] = base_ref[:K, :] + sign * seen[:K]
        flat[K:, :] = base_ref[K:, :] - sign * seen[K:]
        each_owner(lambda i, where: scatter(i, where).start())

    def combine():
        @pl.when(reducing)
        def _():
            parts[me] = flat[rows_of(mine)]
            whole(parts.at[pl.ds(0, n - 1)], recv_c)
            if n <= 64:
                value = parts[0]
                for k in range(1, n):
                    value = value + parts[k]
            else:
                value = lax.fori_loop(1, n, lambda k, acc: acc + parts[k], parts[0])
            total[rows_of(mine)] = value
            each_other(lambda k, where: gather(k, where).start())

    def tip_system():
        owned(total, recv_d)
        work_k[:, :T] = total[:K, :] + tprior_ref[...] * eye(T)
        work_k[:, T:] = eye(T)

    upper = upper_mask(T)

    def odd_gram(c):
        def job():
            at = slice(c * T, (c + 1) * T)
            wide = (lax.broadcasted_iota(jnp.int32, (T, B), 0) + c * T) == lax.broadcasted_iota(jnp.int32, (T, B), 1)
            blk_ref[at, :] = dot(odd_rows[:, at], odd_rows[...], TN) + jnp.where(wide, prior_ref[1:2, :], 0.0)

        return job

    def solve_jobs(b, inv_s):
        at = slice(b * T, (b + 1) * T)

        def fill():
            w_ref[at, :] = mm3(inv_s, split2(w_ref[at, :]), NN)

        def side(rows):
            def job():
                y_ref[rows, at] = mm3(split2(y_ref[rows, at]), inv_s, NT)

            return job

        def send():
            @pl.when(me > 0)
            def _():
                for copy in shift(b):
                    copy.start()

        return [fill, side(slice(B, None)), send, side(slice(0, B))]

    def remainder_jobs(b, rest):
        lo, hi = b * T, (b + 1) * T

        def keep():
            l_ref[hi:, lo:hi] = rest.T

        def update(c):
            def job():
                at, to = slice(hi + c * T, hi + (c + 1) * T), slice(hi + c * T if c else hi + T, None)
                far = rest[:, c * T if c else T :]
                gram[at, to] = gram[at, to] - dot(rest[:, c * T : (c + 1) * T], far, TN)

            return job

        return [update(c) for c in range(nb - 1 - b) if c or b + 2 < nb] + [keep]

    def update_jobs(b, rest_s):
        at, after = slice(b * T, (b + 1) * T), slice((b + 1) * T, None)

        def fill():
            w_ref[after, :] = w_ref[after, :] - mm3(rest_s, split2(w_ref[at, :]), TN)

        def side(rows):
            def job():
                y_ref[rows, after] = y_ref[rows, after] - mm3(split2(y_ref[rows, at]), rest_s, NN)

            return job

        return [fill, side(slice(B, None)), side(slice(0, B))]

    def product_jobs(b):
        at = slice(b * T, (b + 1) * T)

        def square(c):
            def job():
                rows = slice(c * T, (c + 1) * T)
                blk_ref[rows, :] = blk_ref[rows, :] - mm3(split2(y_ref[rows, at]), split2(y_ref[:B, at]), NT)

            return job

        def link(c):
            def job():
                rows = slice(c * T, (c + 1) * T)
                value = mm3(split2(y_ref[rows, at]), split2(w_ref[at, :]), NN)
                odd_ref[rows, :] = odd_ref[rows, :] - value if b else -value

            return job

        def side():
            part_ref[...] = part_ref[...] - mm3(split2(y_ref[B:, at]), split2(y_ref[:B, at]), NT)

        return [side] + [square(c) for c in range(nb)] + [link(c) for c in range(nb)]

    def next_jobs(b):
        at = slice(b * T, (b + 1) * T)

        def wait():
            @pl.when(me < n - 1)
            def _():
                for copy in shift(b):
                    copy.wait_recv()

        def square(c):
            def job():
                rows = slice(c * T, (c + 1) * T)
                blk_ref[rows, :] = blk_ref[rows, :] - mm3(split2(nw_ref[at, rows]), split2(nw_ref[at, :]), TN)

            return job

        def side():
            part_ref[...] = part_ref[...] - mm3(split2(ny_ref[:, at]), split2(nw_ref[at, :]), NN)

        return [wait, side] + [square(c) for c in range(nb)]

    jobs = [even_gram(c) for c in range(nb)] + [odd_gram(c) for c in range(nb)]
    inverse = []
    for b in range(nb):
        lo, hi = b * T, (b + 1) * T
        last = b + 1 == nb
        work[:, :T] = gram[lo:hi, lo:hi]
        work[:, T:] = eye(T)
        works = [work]
        if b == 0 and early:
            works = [work, work_k]
        elif b == 1 and early and not last:
            jobs = jobs + [combine]
        factor_tiles(works, jobs)
        if b == 0 and early:
            side = dot(crossed, jnp.where(upper.T, work_k[:, T:], 0.0), NT)
            terms(dot(side, side[:K], NT), 1.0)
        inv_b = jnp.where(upper.T, work[:, T:], 0.0)
        inv_s = split2(inv_b)
        inverse.append(inv_s)
        l_ref[lo:hi, lo:hi] = jnp.where(upper, work[:, :T], 0.0).T
        jobs = solve_jobs(b, inv_s)
        if last:
            for job in jobs:
                job()
            jobs = []
        else:
            rest = dot(inv_b, gram[lo:hi, hi:], NN)
            near = rest[:, :T]
            gram[hi : hi + T, hi : hi + T] = gram[hi : hi + T, hi : hi + T] - dot(near, near, TN)
            jobs = remainder_jobs(b, rest) + jobs + update_jobs(b, split2(rest))
        jobs = jobs + product_jobs(b)
        if b:
            jobs = jobs + next_jobs(b - 1)
    if not early:
        side = y_ref[B:, :]
        terms(dot(side, side[:K], NT), -1.0)
    if not early or nb < 2:
        combine()

    def back_job(b):
        def job():
            at, after = slice(b * T, (b + 1) * T), slice((b + 1) * T, None)
            value = y_ref[B:, at]
            if b + 1 < nb:
                value = value - mm3(split2(back_ref[:, after]), split2(l_ref[after, at]), NN)
            back_ref[:, at] = mm3(split2(value), inverse[b], NN)

        return job

    tip_system()
    factor_tiles([work_k], [back_job(b) for b in reversed(range(nb))] + jobs)
    inv = jnp.where(upper.T, work_k[:, T:], 0.0)
    vec = jnp.concatenate([trhs_ref[...] - total[K : K + 1, :]] * SUB, axis=0)
    sol = dot(dot(vec, inv, NT), inv, NN)
    sol_ref[...] = sol
    res_ref[...] = back_ref[K:, :] - dot(sol, back_ref[:K, :], NN)

    owned(flat, send_c)

    @pl.when(reducing)
    def _():
        whole(parts.at[pl.ds(0, n - 1)], send_d)

    whole(stage.at[pl.ds(1, groups - 1)], send_a)

    whole(landed.at[pl.ds(1, n_obs - 1)], send_b)

    @pl.when(me > 0)
    def _():
        for b in range(nb):
            for copy in shift(b):
                copy.wait_send()

    @pl.when(me < n - 1)
    def _():
        for copy in shift(nb - 1):
            copy.wait_recv()


def last_kernel(
    l_ref, w_ref, y_ref, blk_ref, odd_ref, part_ref, nw_ref, ny_ref, even_ref, tip_ref,
    oblk_ref, olow_ref, otip_ref, res_ref, sol_ref,
    blk, tip, sems,
):
    B = blk_ref.shape[0]
    K = tip_ref.shape[1]
    copies = [
        pltpu.make_async_copy(l_ref, oblk_ref.at[0], sems.at[0]),
        pltpu.make_async_copy(w_ref, olow_ref.at[0], sems.at[1]),
        pltpu.make_async_copy(odd_ref, olow_ref.at[1], sems.at[2]),
        pltpu.make_async_copy(y_ref.at[pl.ds(B, K)], otip_ref.at[0], sems.at[3]),
    ]
    for copy in copies:
        copy.start()
    next_s = split2(nw_ref[B - T :, :])
    blk[...] = blk_ref[...] - mm3(next_s, next_s, TN)
    square = pltpu.make_async_copy(blk, oblk_ref.at[1], sems.at[4])
    square.start()
    right = part_ref[...] - mm3(split2(ny_ref[:, B - T :]), next_s, NN)
    tip[...] = right[:K]
    side = pltpu.make_async_copy(tip, otip_ref.at[1], sems.at[5])
    side.start()
    res_ref[0:1, :] = even_ref[0:1, :]
    res_ref[1:2, :] = right[K : K + 1]
    sol_ref[...] = tip_ref[0:1, :]
    for copy in copies + [square, side]:
        copy.wait()


def vmem(shape):
    return pltpu.VMEM(shape, jnp.float32)


def local(
    obs_rows, obs_owner, obs_member, prior_diag, lower_coupling, tip_coupling, time_rhs, tip_prior, tip_rhs,
):
    groups, members = lax.axis_size("tm"), lax.axis_size("obs")
    n = groups * members
    B = prior_diag.shape[1]
    K = tip_coupling.shape[1]
    nb = B // T
    width = R * B + T
    count = n * CAP * R
    wide = K + SUB
    sems = [10, 1, groups, 1, 1, 1, 1, 1, 1, 2 * nb, 2 * nb]
    held = pl.pallas_call(
        main_kernel,
        out_shape=[
            vmem(s)
            for s in (
                (B, B), (B, B), (B + wide, B), (B, B), (B, B), (wide, B), (B, B), (wide, B), (SUB, B), (SUB, K),
            )
        ],
        in_specs=[HBM] * 9,
        out_specs=[VMEM] * 10,
        scratch_shapes=[
            vmem(obs_rows.shape),
            pltpu.VMEM((1, obs_owner.size), jnp.int32),
            pltpu.VMEM((1, obs_owner.size), jnp.int32),
        ]
        + [
            vmem(s)
            for s in (
                (2, B), (2, K, B), (2, B), (1, K), (1, K), (groups, CAP, width), (groups, CAP, width), (members, groups, CAP, width),
                (count, B), (count, B), (B, B), (T, 2 * T), (T, 2 * T), (wide, K), (n, SUB, K), (wide, K), (wide, K),
                (wide, B),
            )
        ]
        + [pltpu.SemaphoreType.DMA((s,)) for s in sems],
        compiler_params=pltpu.CompilerParams(
            vmem_limit_bytes=40 << 20, collective_id=1, has_side_effects=True
        ),
    )(
        *(
            pltpu.with_memory_space_constraint(x, pltpu.HBM)
            for x in (
                obs_rows, obs_owner.reshape(1, -1), obs_member.reshape(1, -1), prior_diag,
                lower_coupling, tip_coupling, time_rhs, tip_prior[None, :], tip_rhs[None, :],
            )
        )
    )
    block, low, tip, result, sol = pl.pallas_call(
        last_kernel,
        out_shape=[
            jax.ShapeDtypeStruct(s, jnp.float32) for s in ((2, B, B), (2, B, B), (2, K, B), (2, B), (1, K))
        ],
        in_specs=[VMEM] * 10,
        out_specs=[HBM, HBM, HBM, VMEM, VMEM],
        scratch_shapes=[vmem((B, B)), vmem((K, B)), pltpu.SemaphoreType.DMA((6,))],
        compiler_params=pltpu.CompilerParams(vmem_limit_bytes=40 << 20),
    )(*held)
    return block, low, tip, result, sol[0]


def solution(mesh):
    split = ("tm", "obs")
    two, three = P(split, None), P(split, None, None)
    return jax.shard_map(
        local,
        mesh=mesh,
        in_specs=(two, two, two, two, three, three, two, P(), P()),
        out_specs=(three, three, three, two, P()),
        check_vma=False,
    )
```

```python
import jax
import jax.numpy as jnp
from jax import lax
from jax.experimental import pallas as pl
from jax.experimental.pallas import tpu as pltpu
from jax.sharding import PartitionSpec as P

R = 2
CAP = 2
T = 128
PANEL = 32
LEAD = 2
PAIR_LEAD = 1
SUB = 8
HI = lax.Precision.HIGHEST
VMEM = pl.BlockSpec(memory_space=pltpu.VMEM)
HBM = pl.BlockSpec(memory_space=pltpu.HBM)
MESH = pl.DeviceIdType.MESH
NN = (((1,), (0,)), ((), ()))
NT = (((1,), (1,)), ((), ()))
TN = (((0,), (0,)), ((), ()))


def dot(a, b, dims):
    return lax.dot_general(a, b, dims, precision=HI, preferred_element_type=jnp.float32)


def split2(x):
    h = x.astype(jnp.bfloat16)
    return h, (x - h.astype(jnp.float32)).astype(jnp.bfloat16)


def split3(x):
    h = x.astype(jnp.bfloat16)
    rest = x - h.astype(jnp.float32)
    m = rest.astype(jnp.bfloat16)
    return h, m, (rest - m.astype(jnp.float32)).astype(jnp.bfloat16)


def mm3(a, b, dims):
    (ca,), (cb,) = dims[0]
    left = jnp.concatenate([a[0], a[1], a[0]], axis=ca)
    right = jnp.concatenate([b[0], b[0], b[1]], axis=cb)
    return lax.dot_general(left, right, dims, preferred_element_type=jnp.float32)


def panel_gram(rows):
    h, m, l = split3(rows)
    left = jnp.concatenate([part[:, :T] for part in (h, h, m, h, l, m)], axis=0)
    right = jnp.concatenate([h, m, h, l, h, m], axis=0)
    return lax.dot_general(left, right, TN, preferred_element_type=jnp.float32)


def spread(x, i):
    return jnp.broadcast_to(x[i : i + 1, :], x.shape)


def eliminate_strip(left, right, base, first, lead):
    sub = lax.broadcasted_iota(jnp.int32, (SUB, T), 0)
    lane = lax.broadcasted_iota(jnp.int32, (SUB, T), 1)
    size = lead * SUB
    at = base + first * SUB

    def column(g, j):
        return jnp.broadcast_to(jnp.sum(jnp.where(lane == at + j, left[g], 0.0), axis=1, keepdims=True), (SUB, T))

    cols = {(j, g): column(g, j) for j in range(size) for g in range(first, first + lead)}
    scale = [jnp.zeros((SUB, T), jnp.float32) for _ in range(lead)]
    pivots = []
    for i in range(0, size, 2):
        f, s = first + i // SUB, i % SUB
        a, b, c = spread(cols[i, f], s), spread(cols[i + 1, f], s), spread(cols[i + 1, f], s + 1)
        det = a * c - b * b
        inv_det, inv_a = 1.0 / det, 1.0 / a
        pivots.append((a, b, c, inv_det, b * inv_a))
        scale[f - first] = jnp.where(
            sub == s, lax.rsqrt(a), jnp.where(sub == s + 1, lax.rsqrt(det * inv_a), scale[f - first])
        )
        l1, l2 = spread(left[f], s), spread(left[f], s + 1)
        r1, r2 = spread(right[f], s), spread(right[f], s + 1)
        heads = {j: (spread(cols[j, f], s), spread(cols[j, f], s + 1)) for j in range(i + 2, size)}
        for g in range(f, first + lead):
            ci, cj = cols[i, g], cols[i + 1, g]
            n1, n2 = c * ci - b * cj, a * cj - b * ci
            if g == f:
                n1, n2 = jnp.where(sub > s + 1, n1, 0.0), jnp.where(sub > s + 1, n2, 0.0)
            m1, m2 = n1 * inv_det, n2 * inv_det
            if g > f or s + 2 < SUB:
                for j in range(i + 2, size):
                    cols[j, g] = cols[j, g] - m1 * heads[j][0] - m2 * heads[j][1]
            if g == f:
                m1 = jnp.where(sub == s + 1, b * inv_a, m1)
            left[g] = left[g] - m1 * l1 - m2 * l2
            right[g] = right[g] - m1 * r1 - m2 * r2
    for g in range(first + lead, len(left)):
        mine = [column(g, j) for j in range(size)]
        for i in range(0, size, 2):
            f, s = first + i // SUB, i % SUB
            a, b, c, inv_det, link = pivots[i // 2]
            m1 = (c * mine[i] - b * mine[i + 1]) * inv_det
            m2 = (a * mine[i + 1] - b * mine[i]) * inv_det
            for j in range(i + 2, size):
                mine[j] = mine[j] - m1 * spread(cols[j, f], s) - m2 * spread(cols[j, f], s + 1)
            m1 = m1 + m2 * link
            left[g] = left[g] - m1 * spread(left[f], s) - m2 * spread(left[f], s + 1)
            right[g] = right[g] - m1 * spread(right[f], s) - m2 * spread(right[f], s + 1)
    for k in range(lead):
        left[first + k] = left[first + k] * scale[k]
        right[first + k] = right[first + k] * scale[k]


def factor_tiles(works, jobs=()):
    steps = T // PANEL
    lead = LEAD if len(works) == 1 else PAIR_LEAD
    groups = PANEL // SUB
    firsts = range(0, groups, lead)
    slots = steps * len(firsts)
    slot = 0
    for p in range(steps):
        base = p * PANEL
        below = base + PANEL
        sides = []
        for work in works:
            rows = work[base:below, :]
            sides.append(tuple([rows[SUB * g : SUB * (g + 1), h : h + T] for g in range(groups)] for h in (0, T)))
        for first in firsts:
            for left, right in sides:
                eliminate_strip(left, right, base, first, lead)
            if first + lead == groups:
                done = [
                    jnp.concatenate([jnp.concatenate(pair, axis=1) for pair in zip(left, right)], axis=0)
                    for left, right in sides
                ]
                for work, rows in zip(works, done):
                    work[base:below, :] = rows
            for job in jobs[slot * len(jobs) // slots : (slot + 1) * len(jobs) // slots]:
                job()
            slot += 1
        if below < T:
            for work, rows in zip(works, done):
                work[below:, :] = work[below:, :] - panel_gram(rows)[below:, :]


def eye(n):
    return (
        lax.broadcasted_iota(jnp.int32, (n, n), 0) == lax.broadcasted_iota(jnp.int32, (n, n), 1)
    ).astype(jnp.float32)


def upper_mask(n):
    return lax.broadcasted_iota(jnp.int32, (n, n), 0) <= lax.broadcasted_iota(jnp.int32, (n, n), 1)


def pack(rows_ref, owner_ref, member_ref, out_ref):
    groups = out_ref.shape[0]
    blocks, width = rows_ref.shape
    owners = owner_ref[...]
    down = lax.broadcasted_iota(jnp.int32, (blocks, blocks), 0)
    along = lax.broadcasted_iota(jnp.int32, (blocks, blocks), 1)
    wide = jnp.broadcast_to(owners.astype(jnp.float32), (blocks, blocks))
    column = jnp.sum(jnp.where(down == along, wide, 0.0), axis=1, keepdims=True)
    same = jnp.logical_and(column == wide, down < along)
    rank = jnp.sum(same.astype(jnp.int32), axis=0, keepdims=True)
    slot = owners * CAP + rank
    pick = (lax.broadcasted_iota(jnp.int32, (groups * CAP, blocks), 0) == slot).astype(jnp.float32)
    parts = jnp.concatenate([part.astype(jnp.float32) for part in split3(rows_ref[...])], axis=0)
    rows = lax.dot_general(
        jnp.concatenate([pick] * 3, axis=1).astype(jnp.bfloat16), parts.astype(jnp.bfloat16), NN,
        preferred_element_type=jnp.float32,
    )
    tag = jnp.sum(pick * (member_ref[...].astype(jnp.float32) + 1.0), axis=1, keepdims=True)
    tags = jnp.broadcast_to(tag, (groups * CAP, T))
    for g in range(groups):
        out_ref[g, :, :width] = rows[g * CAP : (g + 1) * CAP, :]
        out_ref[g, :, width:] = tags[g * CAP : (g + 1) * CAP, :]


def main_kernel(
    rows_in, owner_in, member_in, prior_in, lower_in, tip_in, rhs_in, tprior_in, trhs_in,
    l_ref, w_ref, y_ref, blk_ref, odd_ref, part_ref, nw_ref, ny_ref, res_ref, sol_ref,
    rows_ref, owner_ref, member_ref, prior_ref, tip, rhs_ref, tprior_ref, trhs_ref, outgoing,
    stage, landed, even_rows, odd_rows, gram, work, work_k, flat, parts, total, base_ref, back_ref,
    local_sem, send_a, recv_a, send_b, recv_b, send_c, recv_c, send_d, recv_d, send_e, recv_e,
):
    groups, n_obs = lax.axis_size("tm"), lax.axis_size("obs")
    n = groups * n_obs
    t, o = lax.axis_index("tm"), lax.axis_index("obs")
    me = t * n_obs + o
    B = prior_ref.shape[1]
    K = tip.shape[1]
    nb = B // T
    chunks = (K + SUB) // SUB
    count = n * CAP * R
    early = count <= T

    def wrap(i, size):
        return jnp.where(i >= size, i - size, i)

    def remote(src, dst, send, recv, where):
        return pltpu.make_async_remote_copy(
            src_ref=src, dst_ref=dst, send_sem=send, recv_sem=recv, device_id=where, device_id_type=MESH
        )

    def whole(ref, sem):
        pltpu.make_async_copy(ref, ref, sem.at[0]).wait()

    def toward(k):
        peer = wrap(t + k, groups)
        return remote(outgoing.at[peer], stage.at[k], send_a.at[0], recv_a.at[k], (peer, o))

    def across(k, j, passed=True):
        source = stage.at[k] if passed else outgoing.at[t]
        return remote(source, landed.at[j, k], send_b.at[0], recv_b.at[0], (t, wrap(o + j, n_obs)))

    owners = [i * n // chunks for i in range(chunks)]
    mine = (me * chunks + n - 1) // n
    reducing = jnp.logical_and(mine < chunks, mine * n // chunks == me)

    def rows_of(i):
        return pl.ds(pl.multiple_of(i * SUB, SUB), SUB)

    def each_owner(act):
        for i, owner in enumerate(owners):

            @pl.when(me != owner)
            def _():
                act(i, (owner // n_obs, owner % n_obs))

    def scatter(i, where):
        return remote(flat.at[pl.ds(i * SUB, SUB)], parts.at[me], send_c.at[0], recv_c.at[0], where)

    def owned(ref, sem):
        @pl.when(reducing)
        def _():
            whole(ref.at[pl.ds(0, (chunks - 1) * SUB)], sem)

        @pl.when(jnp.logical_not(reducing))
        def _():
            whole(ref, sem)

    def each_other(act):
        @pl.loop(0, groups)
        def _(i):
            for j in range(n_obs):
                k = i * n_obs + j

                @pl.when(k != me)
                def _():
                    act(k, (i, j))

    def gather(k, where):
        rows = rows_of(mine)
        return remote(total.at[rows], total.at[rows], send_d.at[0], recv_d.at[0], where)

    before = (jnp.where(o > 0, t, wrap(t + groups - 1, groups)), wrap(o + n_obs - 1, n_obs))

    def shift(b):
        rows, lanes = pl.ds(b * T, T), pl.ds(b * T, T)
        return (
            remote(w_ref.at[rows], nw_ref.at[rows], send_e.at[2 * b], recv_e.at[2 * b], before),
            remote(
                y_ref.at[pl.ds(B, K + SUB), lanes], ny_ref.at[:, lanes],
                send_e.at[2 * b + 1], recv_e.at[2 * b + 1], before,
            ),
        )

    barrier = pltpu.get_barrier_semaphore()
    pairs = [
        (rows_in, rows_ref), (owner_in, owner_ref), (member_in, member_ref), (prior_in, prior_ref),
        (rhs_in, rhs_ref), (tprior_in, tprior_ref), (trhs_in, trhs_ref), (tip_in, tip), (lower_in.at[0], w_ref), (lower_in.at[1], y_ref.at[pl.ds(0, B)]),
    ]
    loads = [pltpu.make_async_copy(src, dst, local_sem.at[i]) for i, (src, dst) in enumerate(pairs)]
    for load in loads:
        load.start()

    @pl.loop(1, groups)
    def _(k):
        pl.semaphore_signal(barrier, inc=1, device_id=(wrap(t + k, groups), o), device_id_type=MESH)

    for j in range(1, n_obs):
        pl.semaphore_signal(barrier, inc=1, device_id=(t, wrap(o + j, n_obs)), device_id_type=MESH)
    for load in loads[:3]:
        load.wait()
    pack(rows_ref, owner_ref, member_ref, outgoing)
    pl.semaphore_wait(barrier, groups + n_obs - 2)

    @pl.loop(1, groups)
    def _(k):
        toward(k).start()

    for j in range(1, n_obs):
        across(0, j, False).start()

    @pl.loop(1, groups)
    def _(k):
        toward(k).wait_recv()
        for j in range(1, n_obs):
            across(k, j).start()

    for load in loads[3:]:
        load.wait()

    @pl.when(me == 0)
    def _():
        w_ref[...] = jnp.zeros((B, B), jnp.float32)

    y_ref[B : B + K, :] = tip[0]
    y_ref[B + K :, :] = jnp.concatenate([rhs_ref[0:1, :], jnp.zeros((SUB - 1, B), jnp.float32)], axis=0)
    part_ref[:K, :] = tip[1]
    part_ref[K:, :] = jnp.concatenate([rhs_ref[1:2, :], jnp.zeros((SUB - 1, B), jnp.float32)], axis=0)
    root = lax.rsqrt(prior_ref[0:1, :])
    scaled = y_ref[B:, :] * root
    both = dot(tip[0], tip[0], NT) + dot(tip[1], tip[1], NT)
    if early:
        inner = dot(scaled, scaled[:K], NT)
        base_ref[:K, :] = both - inner[:K]
        base_ref[K:, :] = inner[K:]
    else:
        base_ref[:K, :] = both
        base_ref[K:, :] = jnp.zeros((SUB, K), jnp.float32)
    for b in range(nb - 1):
        l_ref[b * T : (b + 1) * T, (b + 1) * T :] = jnp.zeros((T, B - (b + 1) * T), jnp.float32)

    @pl.when(me == n - 1)
    def _():
        nw_ref[...] = jnp.zeros((B, B), jnp.float32)
        ny_ref[...] = jnp.zeros((K + SUB, B), jnp.float32)

    whole(landed.at[pl.ds(1, n_obs - 1)], recv_b)

    even = (2 * o + 1).astype(jnp.float32)
    odd = even + 1.0
    each = SUB // CAP
    pieces = [(j, k) for j in range(n_obs) for k in range(groups)]
    for q in range(0, n, each):
        block = jnp.concatenate([landed[j, k] if j else stage[k] if k else outgoing[t] for j, k in pieces[q : q + each]], axis=0)
        tag = block[:, R * B :]
        for r in range(R):
            at = r * n * CAP + q * CAP
            for c in range(nb):
                x = block[:, r * B + c * T : r * B + (c + 1) * T]
                even_rows[at : at + SUB, c * T : (c + 1) * T] = jnp.where(tag == even, x, 0.0)
                odd_rows[at : at + SUB, c * T : (c + 1) * T] = jnp.where(tag == odd, x, 0.0)
    chosen = even_rows[...]
    gram[:T, :T] = dot(even_rows[:, :T], even_rows[:, :T], TN) + prior_ref[0:1, :T] * eye(T)
    if early:
        weighed = chosen * root
        if count < T:
            weighed = jnp.concatenate([weighed, jnp.zeros((T - count, B), jnp.float32)], axis=0)
        work_k[:, :T] = dot(weighed, weighed, NT) + eye(T)
        work_k[:, T:] = eye(T)
        crossed = dot(scaled, weighed, NT)

    def even_gram(c):
        def job():
            at, to = slice(c * T, (c + 1) * T), slice(c * T if c else T, None)
            value = dot(even_rows[:, at], even_rows[:, to], TN)
            if c:
                wide = lax.broadcasted_iota(jnp.int32, value.shape, 0) == lax.broadcasted_iota(
                    jnp.int32, value.shape, 1
                )
                value = value + jnp.where(wide, prior_ref[0:1, to], 0.0)
            gram[at, to] = value

        return job

    def terms(seen, sign):
        flat[:K, :] = base_ref[:K, :] + sign * seen[:K]
        flat[K:, :] = base_ref[K:, :] - sign * seen[K:]
        each_owner(lambda i, where: scatter(i, where).start())

    def combine():
        @pl.when(reducing)
        def _():
            parts[me] = flat[rows_of(mine)]
            whole(parts.at[pl.ds(0, n - 1)], recv_c)
            if n <= 64:
                value = parts[0]
                for k in range(1, n):
                    value = value + parts[k]
            else:
                value = lax.fori_loop(1, n, lambda k, acc: acc + parts[k], parts[0])
            total[rows_of(mine)] = value
            each_other(lambda k, where: gather(k, where).start())

    def tip_system():
        owned(total, recv_d)
        work_k[:, :T] = total[:K, :] + tprior_ref[...] * eye(T)
        work_k[:, T:] = eye(T)

    upper = upper_mask(T)

    def odd_gram(c):
        def job():
            at = slice(c * T, (c + 1) * T)
            wide = (lax.broadcasted_iota(jnp.int32, (T, B), 0) + c * T) == lax.broadcasted_iota(jnp.int32, (T, B), 1)
            blk_ref[at, :] = dot(odd_rows[:, at], odd_rows[...], TN) + jnp.where(wide, prior_ref[1:2, :], 0.0)

        return job

    def solve_jobs(b, inv_s):
        at = slice(b * T, (b + 1) * T)

        def fill():
            w_ref[at, :] = mm3(inv_s, split2(w_ref[at, :]), NN)

        def side(rows):
            def job():
                y_ref[rows, at] = mm3(split2(y_ref[rows, at]), inv_s, NT)

            return job

        def send():
            @pl.when(me > 0)
            def _():
                for copy in shift(b):
                    copy.start()

        return [fill, side(slice(B, None)), send, side(slice(0, B))]

    def remainder_jobs(b, rest):
        lo, hi = b * T, (b + 1) * T

        def keep():
            l_ref[hi:, lo:hi] = rest.T

        def update(c):
            def job():
                at, to = slice(hi + c * T, hi + (c + 1) * T), slice(hi + c * T if c else hi + T, None)
                far = rest[:, c * T if c else T :]
                gram[at, to] = gram[at, to] - dot(rest[:, c * T : (c + 1) * T], far, TN)

            return job

        return [update(c) for c in range(nb - 1 - b) if c or b + 2 < nb] + [keep]

    def update_jobs(b, rest_s):
        at, after = slice(b * T, (b + 1) * T), slice((b + 1) * T, None)

        def fill():
            w_ref[after, :] = w_ref[after, :] - mm3(rest_s, split2(w_ref[at, :]), TN)

        def side(rows):
            def job():
                y_ref[rows, after] = y_ref[rows, after] - mm3(split2(y_ref[rows, at]), rest_s, NN)

            return job

        return [fill, side(slice(B, None)), side(slice(0, B))]

    def product_jobs(b):
        at = slice(b * T, (b + 1) * T)

        def square(c):
            def job():
                rows = slice(c * T, (c + 1) * T)
                blk_ref[rows, :] = blk_ref[rows, :] - mm3(split2(y_ref[rows, at]), split2(y_ref[:B, at]), NT)

            return job

        def link(c):
            def job():
                rows = slice(c * T, (c + 1) * T)
                value = mm3(split2(y_ref[rows, at]), split2(w_ref[at, :]), NN)
                odd_ref[rows, :] = odd_ref[rows, :] - value if b else -value

            return job

        def side():
            part_ref[...] = part_ref[...] - mm3(split2(y_ref[B:, at]), split2(y_ref[:B, at]), NT)

        return [side] + [square(c) for c in range(nb)] + [link(c) for c in range(nb)]

    def next_jobs(b):
        at = slice(b * T, (b + 1) * T)

        def wait():
            @pl.when(me < n - 1)
            def _():
                for copy in shift(b):
                    copy.wait_recv()

        def square(c):
            def job():
                rows = slice(c * T, (c + 1) * T)
                blk_ref[rows, :] = blk_ref[rows, :] - mm3(split2(nw_ref[at, rows]), split2(nw_ref[at, :]), TN)

            return job

        def side():
            part_ref[...] = part_ref[...] - mm3(split2(ny_ref[:, at]), split2(nw_ref[at, :]), NN)

        return [wait, side] + [square(c) for c in range(nb)]

    jobs = [even_gram(c) for c in range(nb)] + [odd_gram(c) for c in range(nb)]
    inverse = []
    for b in range(nb):
        lo, hi = b * T, (b + 1) * T
        last = b + 1 == nb
        work[:, :T] = gram[lo:hi, lo:hi]
        work[:, T:] = eye(T)
        works = [work]
        if b == 0 and early:
            works = [work, work_k]
        elif b == 1 and early and not last:
            jobs = jobs + [combine]
        factor_tiles(works, jobs)
        if b == 0 and early:
            side = dot(crossed, jnp.where(upper.T, work_k[:, T:], 0.0), NT)
            terms(dot(side, side[:K], NT), 1.0)
        inv_b = jnp.where(upper.T, work[:, T:], 0.0)
        inv_s = split2(inv_b)
        inverse.append(inv_s)
        l_ref[lo:hi, lo:hi] = jnp.where(upper, work[:, :T], 0.0).T
        jobs = solve_jobs(b, inv_s)
        if last:
            for job in jobs:
                job()
            jobs = []
        else:
            rest = dot(inv_b, gram[lo:hi, hi:], NN)
            near = rest[:, :T]
            gram[hi : hi + T, hi : hi + T] = gram[hi : hi + T, hi : hi + T] - dot(near, near, TN)
            jobs = remainder_jobs(b, rest) + jobs + update_jobs(b, split2(rest))
        jobs = jobs + product_jobs(b)
        if b:
            jobs = jobs + next_jobs(b - 1)
    if not early:
        side = y_ref[B:, :]
        terms(dot(side, side[:K], NT), -1.0)
    if not early or nb < 2:
        combine()

    def back_job(b):
        def job():
            at, after = slice(b * T, (b + 1) * T), slice((b + 1) * T, None)
            value = y_ref[B:, at]
            if b + 1 < nb:
                value = value - mm3(split2(back_ref[:, after]), split2(l_ref[after, at]), NN)
            back_ref[:, at] = mm3(split2(value), inverse[b], NN)

        return job

    tip_system()
    factor_tiles([work_k], [back_job(b) for b in reversed(range(nb))] + jobs)
    inv = jnp.where(upper.T, work_k[:, T:], 0.0)
    vec = jnp.concatenate([trhs_ref[...] - total[K : K + 1, :]] * SUB, axis=0)
    sol = dot(dot(vec, inv, NT), inv, NN)
    sol_ref[...] = sol
    res_ref[...] = back_ref[K:, :] - dot(sol, back_ref[:K, :], NN)

    owned(flat, send_c)

    @pl.when(reducing)
    def _():
        whole(parts.at[pl.ds(0, n - 1)], send_d)

    whole(stage.at[pl.ds(1, groups - 1)], send_a)

    whole(landed.at[pl.ds(1, n_obs - 1)], send_b)

    @pl.when(me > 0)
    def _():
        for b in range(nb):
            for copy in shift(b):
                copy.wait_send()

    @pl.when(me < n - 1)
    def _():
        for copy in shift(nb - 1):
            copy.wait_recv()


def last_kernel(
    l_ref, w_ref, y_ref, blk_ref, odd_ref, part_ref, nw_ref, ny_ref, even_ref, tip_ref,
    oblk_ref, olow_ref, otip_ref, res_ref, sol_ref,
    blk, tip, sems,
):
    B = blk_ref.shape[0]
    K = tip_ref.shape[1]
    copies = [
        pltpu.make_async_copy(l_ref, oblk_ref.at[0], sems.at[0]),
        pltpu.make_async_copy(w_ref, olow_ref.at[0], sems.at[1]),
        pltpu.make_async_copy(odd_ref, olow_ref.at[1], sems.at[2]),
        pltpu.make_async_copy(y_ref.at[pl.ds(B, K)], otip_ref.at[0], sems.at[3]),
    ]
    for copy in copies:
        copy.start()
    next_s = split2(nw_ref[B - T :, :])
    blk[...] = blk_ref[...] - mm3(next_s, next_s, TN)
    square = pltpu.make_async_copy(blk, oblk_ref.at[1], sems.at[4])
    square.start()
    right = part_ref[...] - mm3(split2(ny_ref[:, B - T :]), next_s, NN)
    tip[...] = right[:K]
    side = pltpu.make_async_copy(tip, otip_ref.at[1], sems.at[5])
    side.start()
    res_ref[0:1, :] = even_ref[0:1, :]
    res_ref[1:2, :] = right[K : K + 1]
    sol_ref[...] = tip_ref[0:1, :]
    for copy in copies + [square, side]:
        copy.wait()


def vmem(shape):
    return pltpu.VMEM(shape, jnp.float32)


def local(
    obs_rows, obs_owner, obs_member, prior_diag, lower_coupling, tip_coupling, time_rhs, tip_prior, tip_rhs,
):
    groups, members = lax.axis_size("tm"), lax.axis_size("obs")
    n = groups * members
    B = prior_diag.shape[1]
    K = tip_coupling.shape[1]
    nb = B // T
    width = R * B + T
    count = n * CAP * R
    wide = K + SUB
    sems = [10, 1, groups, 1, 1, 1, 1, 1, 1, 2 * nb, 2 * nb]
    held = pl.pallas_call(
        main_kernel,
        out_shape=[
            vmem(s)
            for s in (
                (B, B), (B, B), (B + wide, B), (B, B), (B, B), (wide, B), (B, B), (wide, B), (SUB, B), (SUB, K),
            )
        ],
        in_specs=[HBM] * 9,
        out_specs=[VMEM] * 10,
        scratch_shapes=[
            vmem(obs_rows.shape),
            pltpu.VMEM((1, obs_owner.size), jnp.int32),
            pltpu.VMEM((1, obs_owner.size), jnp.int32),
        ]
        + [
            vmem(s)
            for s in (
                (2, B), (2, K, B), (2, B), (1, K), (1, K), (groups, CAP, width), (groups, CAP, width), (members, groups, CAP, width),
                (count, B), (count, B), (B, B), (T, 2 * T), (T, 2 * T), (wide, K), (n, SUB, K), (wide, K), (wide, K),
                (wide, B),
            )
        ]
        + [pltpu.SemaphoreType.DMA((s,)) for s in sems],
        compiler_params=pltpu.CompilerParams(
            vmem_limit_bytes=40 << 20, collective_id=1, has_side_effects=True
        ),
    )(
        *(
            pltpu.with_memory_space_constraint(x, pltpu.HBM)
            for x in (
                obs_rows, obs_owner.reshape(1, -1), obs_member.reshape(1, -1), prior_diag,
                lower_coupling, tip_coupling, time_rhs, tip_prior[None, :], tip_rhs[None, :],
            )
        )
    )
    block, low, tip, result, sol = pl.pallas_call(
        last_kernel,
        out_shape=[
            jax.ShapeDtypeStruct(s, jnp.float32) for s in ((2, B, B), (2, B, B), (2, K, B), (2, B), (1, K))
        ],
        in_specs=[VMEM] * 10,
        out_specs=[HBM, HBM, HBM, VMEM, VMEM],
        scratch_shapes=[vmem((B, B)), vmem((K, B)), pltpu.SemaphoreType.DMA((6,))],
        compiler_params=pltpu.CompilerParams(vmem_limit_bytes=40 << 20),
    )(*held)
    return block, low, tip, result, sol[0]


def solution(mesh):
    split = ("tm", "obs")
    two, three = P(split, None), P(split, None, None)
    return jax.shard_map(
        local,
        mesh=mesh,
        in_specs=(two, two, two, two, three, three, two, P(), P()),
        out_specs=(three, three, three, two, P()),
        check_vma=False,
    )
```

```python
import jax
import jax.numpy as jnp
from jax import lax
from jax.experimental import pallas as pl
from jax.experimental.pallas import tpu as pltpu
from jax.sharding import PartitionSpec as P

R = 2
CAP = 2
T = 128
PANEL = 32
LEAD = 2
PAIR_LEAD = 1
SUB = 8
HI = lax.Precision.HIGHEST
VMEM = pl.BlockSpec(memory_space=pltpu.VMEM)
HBM = pl.BlockSpec(memory_space=pltpu.HBM)
MESH = pl.DeviceIdType.MESH
NN = (((1,), (0,)), ((), ()))
NT = (((1,), (1,)), ((), ()))
TN = (((0,), (0,)), ((), ()))


def dot(a, b, dims):
    return lax.dot_general(a, b, dims, precision=HI, preferred_element_type=jnp.float32)


def split2(x):
    h = x.astype(jnp.bfloat16)
    return h, (x - h.astype(jnp.float32)).astype(jnp.bfloat16)


def split3(x):
    h = x.astype(jnp.bfloat16)
    rest = x - h.astype(jnp.float32)
    m = rest.astype(jnp.bfloat16)
    return h, m, (rest - m.astype(jnp.float32)).astype(jnp.bfloat16)


def mm3(a, b, dims):
    (ca,), (cb,) = dims[0]
    left = jnp.concatenate([a[0], a[1], a[0]], axis=ca)
    right = jnp.concatenate([b[0], b[0], b[1]], axis=cb)
    return lax.dot_general(left, right, dims, preferred_element_type=jnp.float32)


def panel_gram(rows):
    h, m, l = split3(rows)
    left = jnp.concatenate([part[:, :T] for part in (h, h, m, h, l, m)], axis=0)
    right = jnp.concatenate([h, m, h, l, h, m], axis=0)
    return lax.dot_general(left, right, TN, preferred_element_type=jnp.float32)


def spread(x, i):
    return jnp.broadcast_to(x[i : i + 1, :], x.shape)


def eliminate_strip(left, right, base, first, lead):
    sub = lax.broadcasted_iota(jnp.int32, (SUB, T), 0)
    lane = lax.broadcasted_iota(jnp.int32, (SUB, T), 1)
    size = lead * SUB
    at = base + first * SUB

    def column(g, j):
        return jnp.broadcast_to(jnp.sum(jnp.where(lane == at + j, left[g], 0.0), axis=1, keepdims=True), (SUB, T))

    cols = {(j, g): column(g, j) for j in range(size) for g in range(first, first + lead)}
    scale = [jnp.zeros((SUB, T), jnp.float32) for _ in range(lead)]
    pivots = []
    for i in range(0, size, 2):
        f, s = first + i // SUB, i % SUB
        a, b, c = spread(cols[i, f], s), spread(cols[i + 1, f], s), spread(cols[i + 1, f], s + 1)
        det = a * c - b * b
        inv_det, inv_a = 1.0 / det, 1.0 / a
        pivots.append((a, b, c, inv_det, b * inv_a))
        scale[f - first] = jnp.where(
            sub == s, lax.rsqrt(a), jnp.where(sub == s + 1, lax.rsqrt(det * inv_a), scale[f - first])
        )
        l1, l2 = spread(left[f], s), spread(left[f], s + 1)
        r1, r2 = spread(right[f], s), spread(right[f], s + 1)
        heads = {j: (spread(cols[j, f], s), spread(cols[j, f], s + 1)) for j in range(i + 2, size)}
        for g in range(f, first + lead):
            ci, cj = cols[i, g], cols[i + 1, g]
            n1, n2 = c * ci - b * cj, a * cj - b * ci
            if g == f:
                n1, n2 = jnp.where(sub > s + 1, n1, 0.0), jnp.where(sub > s + 1, n2, 0.0)
            m1, m2 = n1 * inv_det, n2 * inv_det
            if g > f or s + 2 < SUB:
                for j in range(i + 2, size):
                    cols[j, g] = cols[j, g] - m1 * heads[j][0] - m2 * heads[j][1]
            if g == f:
                m1 = jnp.where(sub == s + 1, b * inv_a, m1)
            left[g] = left[g] - m1 * l1 - m2 * l2
            right[g] = right[g] - m1 * r1 - m2 * r2
    for g in range(first + lead, len(left)):
        mine = [column(g, j) for j in range(size)]
        for i in range(0, size, 2):
            f, s = first + i // SUB, i % SUB
            a, b, c, inv_det, link = pivots[i // 2]
            m1 = (c * mine[i] - b * mine[i + 1]) * inv_det
            m2 = (a * mine[i + 1] - b * mine[i]) * inv_det
            for j in range(i + 2, size):
                mine[j] = mine[j] - m1 * spread(cols[j, f], s) - m2 * spread(cols[j, f], s + 1)
            m1 = m1 + m2 * link
            left[g] = left[g] - m1 * spread(left[f], s) - m2 * spread(left[f], s + 1)
            right[g] = right[g] - m1 * spread(right[f], s) - m2 * spread(right[f], s + 1)
    for k in range(lead):
        left[first + k] = left[first + k] * scale[k]
        right[first + k] = right[first + k] * scale[k]


def factor_tiles(works, jobs=()):
    steps = T // PANEL
    lead = LEAD if len(works) == 1 else PAIR_LEAD
    groups = PANEL // SUB
    firsts = range(0, groups, lead)
    slots = steps * len(firsts)
    slot = 0
    for p in range(steps):
        base = p * PANEL
        below = base + PANEL
        sides = []
        for work in works:
            rows = work[base:below, :]
            sides.append(tuple([rows[SUB * g : SUB * (g + 1), h : h + T] for g in range(groups)] for h in (0, T)))
        for first in firsts:
            for left, right in sides:
                eliminate_strip(left, right, base, first, lead)
            if first + lead == groups:
                done = [
                    jnp.concatenate([jnp.concatenate(pair, axis=1) for pair in zip(left, right)], axis=0)
                    for left, right in sides
                ]
                for work, rows in zip(works, done):
                    work[base:below, :] = rows
            for job in jobs[slot * len(jobs) // slots : (slot + 1) * len(jobs) // slots]:
                job()
            slot += 1
        if below < T:
            for work, rows in zip(works, done):
                work[below:, :] = work[below:, :] - panel_gram(rows)[below:, :]


def eye(n):
    return (
        lax.broadcasted_iota(jnp.int32, (n, n), 0) == lax.broadcasted_iota(jnp.int32, (n, n), 1)
    ).astype(jnp.float32)


def upper_mask(n):
    return lax.broadcasted_iota(jnp.int32, (n, n), 0) <= lax.broadcasted_iota(jnp.int32, (n, n), 1)


def pack(rows_ref, owner_ref, member_ref, out_ref):
    groups = out_ref.shape[0]
    blocks, width = rows_ref.shape
    owners = owner_ref[...]
    down = lax.broadcasted_iota(jnp.int32, (blocks, blocks), 0)
    along = lax.broadcasted_iota(jnp.int32, (blocks, blocks), 1)
    wide = jnp.broadcast_to(owners.astype(jnp.float32), (blocks, blocks))
    column = jnp.sum(jnp.where(down == along, wide, 0.0), axis=1, keepdims=True)
    same = jnp.logical_and(column == wide, down < along)
    rank = jnp.sum(same.astype(jnp.int32), axis=0, keepdims=True)
    slot = owners * CAP + rank
    pick = (lax.broadcasted_iota(jnp.int32, (groups * CAP, blocks), 0) == slot).astype(jnp.float32)
    parts = jnp.concatenate([part.astype(jnp.float32) for part in split3(rows_ref[...])], axis=0)
    rows = lax.dot_general(
        jnp.concatenate([pick] * 3, axis=1).astype(jnp.bfloat16), parts.astype(jnp.bfloat16), NN,
        preferred_element_type=jnp.float32,
    )
    tag = jnp.sum(pick * (member_ref[...].astype(jnp.float32) + 1.0), axis=1, keepdims=True)
    tags = jnp.broadcast_to(tag, (groups * CAP, T))
    for g in range(groups):
        out_ref[g, :, :width] = rows[g * CAP : (g + 1) * CAP, :]
        out_ref[g, :, width:] = tags[g * CAP : (g + 1) * CAP, :]


def main_kernel(
    rows_in, owner_in, member_in, prior_in, lower_in, tip_in, rhs_in, tprior_in, trhs_in,
    l_ref, w_ref, y_ref, blk_ref, odd_ref, part_ref, nw_ref, ny_ref, res_ref, sol_ref,
    rows_ref, owner_ref, member_ref, prior_ref, tip, rhs_ref, tprior_ref, trhs_ref, outgoing,
    stage, landed, even_rows, odd_rows, gram, work, work_k, flat, parts, total, base_ref, back_ref,
    local_sem, send_a, recv_a, send_b, recv_b, send_c, recv_c, send_d, recv_d, send_e, recv_e,
):
    groups, n_obs = lax.axis_size("tm"), lax.axis_size("obs")
    n = groups * n_obs
    t, o = lax.axis_index("tm"), lax.axis_index("obs")
    me = t * n_obs + o
    B = prior_ref.shape[1]
    K = tip.shape[1]
    nb = B // T
    chunks = (K + SUB) // SUB
    count = n * CAP * R
    early = count <= T

    def wrap(i, size):
        return jnp.where(i >= size, i - size, i)

    def remote(src, dst, send, recv, where):
        return pltpu.make_async_remote_copy(
            src_ref=src, dst_ref=dst, send_sem=send, recv_sem=recv, device_id=where, device_id_type=MESH
        )

    def whole(ref, sem):
        pltpu.make_async_copy(ref, ref, sem.at[0]).wait()

    def toward(k):
        peer = wrap(t + k, groups)
        return remote(outgoing.at[peer], stage.at[k], send_a.at[0], recv_a.at[k], (peer, o))

    def across(k, j, passed=True):
        source = stage.at[k] if passed else outgoing.at[t]
        return remote(source, landed.at[j, k], send_b.at[0], recv_b.at[0], (t, wrap(o + j, n_obs)))

    owners = [i * n // chunks for i in range(chunks)]
    mine = (me * chunks + n - 1) // n
    reducing = jnp.logical_and(mine < chunks, mine * n // chunks == me)

    def rows_of(i):
        return pl.ds(pl.multiple_of(i * SUB, SUB), SUB)

    def each_owner(act):
        for i, owner in enumerate(owners):

            @pl.when(me != owner)
            def _():
                act(i, (owner // n_obs, owner % n_obs))

    def scatter(i, where):
        return remote(flat.at[pl.ds(i * SUB, SUB)], parts.at[me], send_c.at[0], recv_c.at[0], where)

    def owned(ref, sem):
        @pl.when(reducing)
        def _():
            whole(ref.at[pl.ds(0, (chunks - 1) * SUB)], sem)

        @pl.when(jnp.logical_not(reducing))
        def _():
            whole(ref, sem)

    def each_other(act):
        @pl.loop(0, groups)
        def _(i):
            for j in range(n_obs):
                k = i * n_obs + j

                @pl.when(k != me)
                def _():
                    act(k, (i, j))

    def gather(k, where):
        rows = rows_of(mine)
        return remote(total.at[rows], total.at[rows], send_d.at[0], recv_d.at[0], where)

    before = (jnp.where(o > 0, t, wrap(t + groups - 1, groups)), wrap(o + n_obs - 1, n_obs))

    def shift(b):
        rows, lanes = pl.ds(b * T, T), pl.ds(b * T, T)
        return (
            remote(w_ref.at[rows], nw_ref.at[rows], send_e.at[2 * b], recv_e.at[2 * b], before),
            remote(
                y_ref.at[pl.ds(B, K + SUB), lanes], ny_ref.at[:, lanes],
                send_e.at[2 * b + 1], recv_e.at[2 * b + 1], before,
            ),
        )

    barrier = pltpu.get_barrier_semaphore()
    pairs = [
        (rows_in, rows_ref), (owner_in, owner_ref), (member_in, member_ref), (prior_in, prior_ref),
        (rhs_in, rhs_ref), (tprior_in, tprior_ref), (trhs_in, trhs_ref), (tip_in, tip), (lower_in.at[0], w_ref), (lower_in.at[1], y_ref.at[pl.ds(0, B)]),
    ]
    loads = [pltpu.make_async_copy(src, dst, local_sem.at[i]) for i, (src, dst) in enumerate(pairs)]
    for load in loads:
        load.start()

    @pl.loop(1, groups)
    def _(k):
        pl.semaphore_signal(barrier, inc=1, device_id=(wrap(t + k, groups), o), device_id_type=MESH)

    for j in range(1, n_obs):
        pl.semaphore_signal(barrier, inc=1, device_id=(t, wrap(o + j, n_obs)), device_id_type=MESH)
    for load in loads[:3]:
        load.wait()
    pack(rows_ref, owner_ref, member_ref, outgoing)
    pl.semaphore_wait(barrier, groups + n_obs - 2)

    @pl.loop(1, groups)
    def _(k):
        toward(k).start()

    for j in range(1, n_obs):
        across(0, j, False).start()

    @pl.loop(1, groups)
    def _(k):
        toward(k).wait_recv()
        for j in range(1, n_obs):
            across(k, j).start()

    for load in loads[3:]:
        load.wait()

    @pl.when(me == 0)
    def _():
        w_ref[...] = jnp.zeros((B, B), jnp.float32)

    y_ref[B : B + K, :] = tip[0]
    y_ref[B + K :, :] = jnp.concatenate([rhs_ref[0:1, :], jnp.zeros((SUB - 1, B), jnp.float32)], axis=0)
    part_ref[:K, :] = tip[1]
    part_ref[K:, :] = jnp.concatenate([rhs_ref[1:2, :], jnp.zeros((SUB - 1, B), jnp.float32)], axis=0)
    root = lax.rsqrt(prior_ref[0:1, :])
    scaled = y_ref[B:, :] * root
    both = dot(tip[0], tip[0], NT) + dot(tip[1], tip[1], NT)
    if early:
        inner = dot(scaled, scaled[:K], NT)
        base_ref[:K, :] = both - inner[:K]
        base_ref[K:, :] = inner[K:]
    else:
        base_ref[:K, :] = both
        base_ref[K:, :] = jnp.zeros((SUB, K), jnp.float32)
    for b in range(nb - 1):
        l_ref[b * T : (b + 1) * T, (b + 1) * T :] = jnp.zeros((T, B - (b + 1) * T), jnp.float32)

    @pl.when(me == n - 1)
    def _():
        nw_ref[...] = jnp.zeros((B, B), jnp.float32)
        ny_ref[...] = jnp.zeros((K + SUB, B), jnp.float32)

    whole(landed.at[pl.ds(1, n_obs - 1)], recv_b)

    even = (2 * o + 1).astype(jnp.float32)
    odd = even + 1.0
    each = SUB // CAP
    pieces = [(j, k) for j in range(n_obs) for k in range(groups)]
    for q in range(0, n, each):
        block = jnp.concatenate([landed[j, k] if j else stage[k] if k else outgoing[t] for j, k in pieces[q : q + each]], axis=0)
        tag = block[:, R * B :]
        for r in range(R):
            at = r * n * CAP + q * CAP
            for c in range(nb):
                x = block[:, r * B + c * T : r * B + (c + 1) * T]
                even_rows[at : at + SUB, c * T : (c + 1) * T] = jnp.where(tag == even, x, 0.0)
                odd_rows[at : at + SUB, c * T : (c + 1) * T] = jnp.where(tag == odd, x, 0.0)
    chosen = even_rows[...]
    gram[:T, :T] = dot(even_rows[:, :T], even_rows[:, :T], TN) + prior_ref[0:1, :T] * eye(T)
    if early:
        weighed = chosen * root
        if count < T:
            weighed = jnp.concatenate([weighed, jnp.zeros((T - count, B), jnp.float32)], axis=0)
        work_k[:, :T] = dot(weighed, weighed, NT) + eye(T)
        work_k[:, T:] = eye(T)
        crossed = dot(scaled, weighed, NT)

    def even_gram(c):
        def job():
            at, to = slice(c * T, (c + 1) * T), slice(c * T if c else T, None)
            value = dot(even_rows[:, at], even_rows[:, to], TN)
            if c:
                wide = lax.broadcasted_iota(jnp.int32, value.shape, 0) == lax.broadcasted_iota(
                    jnp.int32, value.shape, 1
                )
                value = value + jnp.where(wide, prior_ref[0:1, to], 0.0)
            gram[at, to] = value

        return job

    def terms(seen, sign):
        flat[:K, :] = base_ref[:K, :] + sign * seen[:K]
        flat[K:, :] = base_ref[K:, :] - sign * seen[K:]
        each_owner(lambda i, where: scatter(i, where).start())

    def combine():
        @pl.when(reducing)
        def _():
            parts[me] = flat[rows_of(mine)]
            whole(parts.at[pl.ds(0, n - 1)], recv_c)
            if n <= 64:
                value = parts[0]
                for k in range(1, n):
                    value = value + parts[k]
            else:
                value = lax.fori_loop(1, n, lambda k, acc: acc + parts[k], parts[0])
            total[rows_of(mine)] = value
            each_other(lambda k, where: gather(k, where).start())

    def tip_system():
        owned(total, recv_d)
        work_k[:, :T] = total[:K, :] + tprior_ref[...] * eye(T)
        work_k[:, T:] = eye(T)

    upper = upper_mask(T)

    def odd_gram(c):
        def job():
            at = slice(c * T, (c + 1) * T)
            wide = (lax.broadcasted_iota(jnp.int32, (T, B), 0) + c * T) == lax.broadcasted_iota(jnp.int32, (T, B), 1)
            blk_ref[at, :] = dot(odd_rows[:, at], odd_rows[...], TN) + jnp.where(wide, prior_ref[1:2, :], 0.0)

        return job

    def solve_jobs(b, inv_s):
        at = slice(b * T, (b + 1) * T)

        def fill():
            w_ref[at, :] = mm3(inv_s, split2(w_ref[at, :]), NN)

        def side(rows):
            def job():
                y_ref[rows, at] = mm3(split2(y_ref[rows, at]), inv_s, NT)

            return job

        def send():
            @pl.when(me > 0)
            def _():
                for copy in shift(b):
                    copy.start()

        return [fill, side(slice(B, None)), send, side(slice(0, B))]

    def remainder_jobs(b, rest):
        lo, hi = b * T, (b + 1) * T

        def keep():
            l_ref[hi:, lo:hi] = rest.T

        def update(c):
            def job():
                at, to = slice(hi + c * T, hi + (c + 1) * T), slice(hi + c * T if c else hi + T, None)
                far = rest[:, c * T if c else T :]
                gram[at, to] = gram[at, to] - dot(rest[:, c * T : (c + 1) * T], far, TN)

            return job

        return [update(c) for c in range(nb - 1 - b) if c or b + 2 < nb] + [keep]

    def update_jobs(b, rest_s):
        at, after = slice(b * T, (b + 1) * T), slice((b + 1) * T, None)

        def fill():
            w_ref[after, :] = w_ref[after, :] - mm3(rest_s, split2(w_ref[at, :]), TN)

        def side(rows):
            def job():
                y_ref[rows, after] = y_ref[rows, after] - mm3(split2(y_ref[rows, at]), rest_s, NN)

            return job

        return [fill, side(slice(B, None)), side(slice(0, B))]

    def product_jobs(b):
        at = slice(b * T, (b + 1) * T)

        def square(c):
            def job():
                rows = slice(c * T, (c + 1) * T)
                blk_ref[rows, :] = blk_ref[rows, :] - mm3(split2(y_ref[rows, at]), split2(y_ref[:B, at]), NT)

            return job

        def link(c):
            def job():
                rows = slice(c * T, (c + 1) * T)
                value = mm3(split2(y_ref[rows, at]), split2(w_ref[at, :]), NN)
                odd_ref[rows, :] = odd_ref[rows, :] - value if b else -value

            return job

        def side():
            part_ref[...] = part_ref[...] - mm3(split2(y_ref[B:, at]), split2(y_ref[:B, at]), NT)

        return [side] + [square(c) for c in range(nb)] + [link(c) for c in range(nb)]

    def next_jobs(b):
        at = slice(b * T, (b + 1) * T)

        def wait():
            @pl.when(me < n - 1)
            def _():
                for copy in shift(b):
                    copy.wait_recv()

        def square(c):
            def job():
                rows = slice(c * T, (c + 1) * T)
                blk_ref[rows, :] = blk_ref[rows, :] - mm3(split2(nw_ref[at, rows]), split2(nw_ref[at, :]), TN)

            return job

        def side():
            part_ref[...] = part_ref[...] - mm3(split2(ny_ref[:, at]), split2(nw_ref[at, :]), NN)

        return [wait, side] + [square(c) for c in range(nb)]

    jobs = [even_gram(c) for c in range(nb)] + [odd_gram(c) for c in range(nb)]
    inverse = []
    for b in range(nb):
        lo, hi = b * T, (b + 1) * T
        last = b + 1 == nb
        work[:, :T] = gram[lo:hi, lo:hi]
        work[:, T:] = eye(T)
        works = [work]
        if b == 0 and early:
            works = [work, work_k]
        elif b == 1 and early and not last:
            jobs = jobs + [combine]
        factor_tiles(works, jobs)
        if b == 0 and early:
            side = dot(crossed, jnp.where(upper.T, work_k[:, T:], 0.0), NT)
            terms(dot(side, side[:K], NT), 1.0)
        inv_b = jnp.where(upper.T, work[:, T:], 0.0)
        inv_s = split2(inv_b)
        inverse.append(inv_s)
        l_ref[lo:hi, lo:hi] = jnp.where(upper, work[:, :T], 0.0).T
        jobs = solve_jobs(b, inv_s)
        if last:
            for job in jobs:
                job()
            jobs = []
        else:
            rest = dot(inv_b, gram[lo:hi, hi:], NN)
            near = rest[:, :T]
            gram[hi : hi + T, hi : hi + T] = gram[hi : hi + T, hi : hi + T] - dot(near, near, TN)
            jobs = remainder_jobs(b, rest) + jobs + update_jobs(b, split2(rest))
        jobs = jobs + product_jobs(b)
        if b:
            jobs = jobs + next_jobs(b - 1)
    if not early:
        side = y_ref[B:, :]
        terms(dot(side, side[:K], NT), -1.0)
    if not early or nb < 2:
        combine()

    def back_job(b):
        def job():
            at, after = slice(b * T, (b + 1) * T), slice((b + 1) * T, None)
            value = y_ref[B:, at]
            if b + 1 < nb:
                value = value - mm3(split2(back_ref[:, after]), split2(l_ref[after, at]), NN)
            back_ref[:, at] = mm3(split2(value), inverse[b], NN)

        return job

    tip_system()
    factor_tiles([work_k], [back_job(b) for b in reversed(range(nb))] + jobs)
    inv = jnp.where(upper.T, work_k[:, T:], 0.0)
    vec = jnp.concatenate([trhs_ref[...] - total[K : K + 1, :]] * SUB, axis=0)
    sol = dot(dot(vec, inv, NT), inv, NN)
    sol_ref[...] = sol
    res_ref[...] = back_ref[K:, :] - dot(sol, back_ref[:K, :], NN)

    owned(flat, send_c)

    @pl.when(reducing)
    def _():
        whole(parts.at[pl.ds(0, n - 1)], send_d)

    whole(stage.at[pl.ds(1, groups - 1)], send_a)

    whole(landed.at[pl.ds(1, n_obs - 1)], send_b)

    @pl.when(me > 0)
    def _():
        for b in range(nb):
            for copy in shift(b):
                copy.wait_send()

    @pl.when(me < n - 1)
    def _():
        for copy in shift(nb - 1):
            copy.wait_recv()


def last_kernel(
    l_ref, w_ref, y_ref, blk_ref, odd_ref, part_ref, nw_ref, ny_ref, even_ref, tip_ref,
    oblk_ref, olow_ref, otip_ref, res_ref, sol_ref,
    blk, tip, res, sol, sems,
):
    B = blk_ref.shape[0]
    K = tip_ref.shape[1]
    copies = [
        pltpu.make_async_copy(l_ref, oblk_ref.at[0], sems.at[0]),
        pltpu.make_async_copy(w_ref, olow_ref.at[0], sems.at[1]),
        pltpu.make_async_copy(odd_ref, olow_ref.at[1], sems.at[2]),
        pltpu.make_async_copy(y_ref.at[pl.ds(B, K)], otip_ref.at[0], sems.at[3]),
    ]
    for copy in copies:
        copy.start()
    next_s = split2(nw_ref[B - T :, :])
    blk[...] = blk_ref[...] - mm3(next_s, next_s, TN)
    square = pltpu.make_async_copy(blk, oblk_ref.at[1], sems.at[4])
    square.start()
    right = part_ref[...] - mm3(split2(ny_ref[:, B - T :]), next_s, NN)
    tip[...] = right[:K]
    side = pltpu.make_async_copy(tip, otip_ref.at[1], sems.at[5])
    side.start()
    res[0:1, :] = even_ref[0:1, :]
    res[1:2, :] = right[K : K + 1]
    sol[...] = tip_ref[0:1, :]
    small = [
        pltpu.make_async_copy(res, res_ref, sems.at[6]),
        pltpu.make_async_copy(sol, sol_ref, sems.at[7]),
    ]
    for copy in small:
        copy.start()
    for copy in copies + [square, side] + small:
        copy.wait()


def vmem(shape):
    return pltpu.VMEM(shape, jnp.float32)


def local(
    obs_rows, obs_owner, obs_member, prior_diag, lower_coupling, tip_coupling, time_rhs, tip_prior, tip_rhs,
):
    groups, members = lax.axis_size("tm"), lax.axis_size("obs")
    n = groups * members
    B = prior_diag.shape[1]
    K = tip_coupling.shape[1]
    nb = B // T
    width = R * B + T
    count = n * CAP * R
    wide = K + SUB
    sems = [10, 1, groups, 1, 1, 1, 1, 1, 1, 2 * nb, 2 * nb]
    held = pl.pallas_call(
        main_kernel,
        out_shape=[
            vmem(s)
            for s in (
                (B, B), (B, B), (B + wide, B), (B, B), (B, B), (wide, B), (B, B), (wide, B), (SUB, B), (SUB, K),
            )
        ],
        in_specs=[HBM] * 9,
        out_specs=[VMEM] * 10,
        scratch_shapes=[
            vmem(obs_rows.shape),
            pltpu.VMEM((1, obs_owner.size), jnp.int32),
            pltpu.VMEM((1, obs_owner.size), jnp.int32),
        ]
        + [
            vmem(s)
            for s in (
                (2, B), (2, K, B), (2, B), (1, K), (1, K), (groups, CAP, width), (groups, CAP, width), (members, groups, CAP, width),
                (count, B), (count, B), (B, B), (T, 2 * T), (T, 2 * T), (wide, K), (n, SUB, K), (wide, K), (wide, K),
                (wide, B),
            )
        ]
        + [pltpu.SemaphoreType.DMA((s,)) for s in sems],
        compiler_params=pltpu.CompilerParams(
            vmem_limit_bytes=40 << 20, collective_id=1, has_side_effects=True
        ),
    )(
        *(
            pltpu.with_memory_space_constraint(x, pltpu.HBM)
            for x in (
                obs_rows, obs_owner.reshape(1, -1), obs_member.reshape(1, -1), prior_diag,
                lower_coupling, tip_coupling, time_rhs, tip_prior[None, :], tip_rhs[None, :],
            )
        )
    )
    block, low, tip, result, sol = pl.pallas_call(
        last_kernel,
        out_shape=[
            jax.ShapeDtypeStruct(s, jnp.float32) for s in ((2, B, B), (2, B, B), (2, K, B), (2, B), (1, K))
        ],
        in_specs=[VMEM] * 10,
        out_specs=[HBM] * 5,
        scratch_shapes=[
            vmem((B, B)), vmem((K, B)), vmem((2, B)), vmem((1, K)), pltpu.SemaphoreType.DMA((8,)),
        ],
        compiler_params=pltpu.CompilerParams(vmem_limit_bytes=40 << 20),
    )(*held)
    return block, low, tip, result, sol[0]


def solution(mesh):
    split = ("tm", "obs")
    two, three = P(split, None), P(split, None, None)
    return jax.shard_map(
        local,
        mesh=mesh,
        in_specs=(two, two, two, two, three, three, two, P(), P()),
        out_specs=(three, three, three, two, P()),
        check_vma=False,
    )
```
